32 devices in a mesh: member: 2 (over y), lat: 4 (over z), lon: 2 (over x), lev: 2 (over core).
Axes of the slice: x: 2, y: 2, z: 4, core: 2. Of those that a mesh axis runs over, the one named last changes fastest.
Arguments:
- adjoint_in: float32 [10, 16, 32, 1152], P('member', 'lev', 'lat', 'lon'), parts along dimension 0, may hold values from -12 to 12
- lat_ahead: float32 [32, 32, 1152], P(('member', 'lev'), 'lat', 'lon'), parts along dimension 0, may hold values from 0.35 to 0.8
- lat_behind: float32 [32, 32, 1152], P(('member', 'lev'), 'lat', 'lon'), parts along dimension 0, may hold values from 0.02 to 0.06
- lon_ahead: float32 [32, 32, 1152], P(('member', 'lev'), 'lat', 'lon'), parts along dimension 0, may hold values from 0.02 to 0.06
- lon_behind: float32 [32, 32, 1152], P(('member', 'lev'), 'lat', 'lon'), parts along dimension 0, may hold values from 0.02 to 0.06
- coupling: float32 [16, 5, 5], P('lev'), may hold values from -0.9 to 0.9
- cutoff: int32 [32], replicated, may hold values from 1 to 576, as said below
Outputs:
- adjoint_out: float32 [10, 16, 32, 1152], P('member', 'lev', 'lat', 'lon'), parts along dimension 0
The draws below stay inside these ranges and needn't reach their ends.
There are 2 independent parts, one for each index of `member`. The reference program is written for one: setup_inputs(seed, part) draws one part's arguments, and reference() takes and returns one part's arrays. A program takes and returns all parts, laid end to end along the dimension named above; an argument that names none is the same for every part. Nothing has to cross between parts.
Inputs may be any that keep to these rules, and one draw needn't show every extreme that they name: Rows 8 to 23 have a cutoff of exactly 576, every other row a cutoff below 576; the first and the last row have cutoff 1.
All inputs are finite; a program needn't handle non-finite values.
Results may differ from the reference program's by a relative error of at most 0.00011.
Values sent between devices are 32-bit elements; how exact they have to be, the bound alone decides.
No kernel may reach another device: no remote copies, remote signals or barrier semaphores. Data moves between devices by JAX's collectives and lax.ppermute only.
A program may use at most 64 MiB of HBM per device.

```python
import math
import jax
import jax.numpy as jnp
from jax import lax

NLON = 1152
FIELDS = 5
SUBSTEPS = 6
NLAT = 32
LEVELS = 16


def draw_cutoff(key, part):
    row_index = jnp.arange(NLAT, dtype=jnp.int32)
    is_polar = (row_index < NLAT // 4) | (row_index >= 3 * NLAT // 4)
    drawn = jax.random.randint(key, (NLAT,), 1, NLON // 2, dtype=jnp.int32)
    drawn = jnp.where((row_index == 0) | (row_index == NLAT - 1), 1, drawn)
    return jnp.where(is_polar, drawn, NLON // 2).astype(jnp.int32)


def level_of(own_key, shape, cuts, least, largest):
    def one(dim, shards_of):
        steps = jax.random.uniform(jax.random.fold_in(jax.random.fold_in(own_key, 6), dim), (shards_of,), jnp.float32, least / len(cuts), largest / len(cuts))
        return jnp.repeat(jnp.exp(steps), shape[dim] // shards_of).reshape((-1,) + (1,) * (len(shape) - dim - 1))

    level = one(*cuts[0])
    for cut in cuts[1:]:
        level = level * one(*cut)
    return level


def centred(own_key, shape, deviation, most, pieces=(), kind=jnp.bfloat16):
    loudness = level_of(own_key, shape, pieces, -0.22, 0.18) if pieces else 1.0
    result = jax.random.normal(own_key, shape, jnp.float32) * deviation * loudness
    return jnp.minimum(jnp.maximum(result, -most), most).astype(kind)


def setup_inputs(seed: int = 0, part: int = 0) -> dict:
    keys = jax.random.split(jax.random.key(seed), 8)
    part_splits = jax.random.split(jax.random.fold_in(keys[7], part), 8)
    adjoint_in = centred(part_splits[0], (FIELDS, LEVELS, NLAT, NLON), 2.0, 12.0, ((1, 2), (2, 4), (3, 2)), jnp.float32)
    lat_ahead = jnp.clip(jnp.exp(math.log(0.8) - 0.82667861 * jax.random.uniform(part_splits[1], (LEVELS, NLAT, NLON), jnp.float32) ** level_of(part_splits[1], (LEVELS, NLAT, NLON), ((0, 2), (1, 4), (2, 2)), -0.2, 0.2)), 0.35, 0.8)
    lat_behind = jnp.clip(jnp.exp(math.log(0.06) - 1.0986123 * jax.random.uniform(part_splits[2], (LEVELS, NLAT, NLON), jnp.float32) ** level_of(part_splits[2], (LEVELS, NLAT, NLON), ((0, 2), (1, 4), (2, 2)), -0.2, 0.2)), 0.02, 0.06)
    lon_ahead = jnp.clip(jnp.exp(math.log(0.06) - 1.0986123 * jax.random.uniform(part_splits[3], (LEVELS, NLAT, NLON), jnp.float32) ** level_of(part_splits[3], (LEVELS, NLAT, NLON), ((0, 2), (1, 4), (2, 2)), -0.2, 0.2)), 0.02, 0.06)
    lon_behind = jnp.clip(jnp.exp(math.log(0.06) - 1.0986123 * jax.random.uniform(part_splits[4], (LEVELS, NLAT, NLON), jnp.float32) ** level_of(part_splits[4], (LEVELS, NLAT, NLON), ((0, 2), (1, 4), (2, 2)), -0.2, 0.2)), 0.02, 0.06)
    coupling = centred(keys[5], (LEVELS, FIELDS, FIELDS), 0.15, 0.9, ((0, 2),), jnp.float32)
    cutoff = draw_cutoff(jax.random.fold_in(keys[7], 71), part)
    return dict(adjoint_in=adjoint_in, lat_ahead=lat_ahead, lat_behind=lat_behind, lon_ahead=lon_ahead, lon_behind=lon_behind, coupling=coupling, cutoff=cutoff)


def damping_table(cutoff):
    wavenumber = jnp.arange(NLON // 2 + 1).astype(jnp.float32)
    limit = cutoff.astype(jnp.float32)[:, None]
    ratio = limit / jnp.maximum(wavenumber, 1.0)[None, :]
    return jnp.where(wavenumber[None, :] > limit, ratio * ratio, 1.0)


def polar_filter(field_block, damping):
    spectra = jnp.fft.rfft(field_block, axis=-1)
    return jnp.fft.irfft(spectra * damping, n=NLON, axis=-1).astype(jnp.float32)


def reference(adjoint_in, lat_ahead, lat_behind, lon_ahead, lon_behind, coupling, cutoff):
    damping = damping_table(cutoff)
    current = jnp.stack([polar_filter(adjoint_in[field_index], damping) for field_index in range(FIELDS)])
    row_mask = (jnp.arange(NLAT) < NLAT - 1).astype(jnp.float32)[None, :, None]
    north_rate = lat_ahead * row_mask
    zero_row = jnp.zeros((LEVELS, 1, NLON), jnp.float32)
    south_rate = jnp.concatenate([zero_row, lat_behind[:, :-1]], axis=1)
    east_rate = lon_ahead
    west_rate = jnp.roll(lon_behind, 1, axis=2)
    zero_plane = jnp.zeros((FIELDS, LEVELS, 1, NLON), jnp.float32)
    for substep in range(SUBSTEPS):
        current = current + jnp.einsum("lgf,glji->flji", coupling, current, precision=lax.Precision.HIGHEST)
        north_side = jnp.concatenate([current[:, :, 1:], zero_plane], axis=2)
        south_side = jnp.concatenate([zero_plane, current[:, :, :-1]], axis=2)
        east_side = jnp.roll(current, -1, axis=3)
        west_side = jnp.roll(current, 1, axis=3)
        current = (current + east_rate * (east_side - current) + west_rate * (west_side - current)
                   + north_rate * (north_side - current) + south_rate * (south_side - current))
    return current
```

```python
import functools
import math

import jax
import jax.numpy as jnp
import numpy as np
from jax import lax
from jax.experimental import pallas as pl
from jax.experimental.pallas import tpu as pltpu
from jax.sharding import PartitionSpec as P

SUBSTEPS = 6
HALO = SUBSTEPS
LANES = 128
CHUNKS = (5,)
VMEM = pl.BlockSpec(memory_space=pltpu.VMEM)
SMEM = pl.BlockSpec(memory_space=pltpu.SMEM)


def split_bf16(values):
    high = values.astype(jnp.bfloat16)
    low = (values - high.astype(jnp.float32)).astype(jnp.bfloat16)
    return high, low


def split_bf16_numpy(values):
    values = values.astype(np.float32)
    high = values.astype(jnp.bfloat16)
    low = (values - high.astype(np.float32)).astype(jnp.bfloat16)
    return high, low


def mode_tables(length):
    ways = length // LANES
    point = np.arange(LANES)[:, None].astype(np.int64)
    column = np.arange(LANES)[None, :].astype(np.int64)
    half = LANES // 2
    wave = np.where(column <= half, column, column - half)
    angle = 2.0 * np.pi * (point * wave % LANES) / LANES
    weight = np.where((column == 0) | (column == half), 1.0 / LANES, 2.0 / LANES)
    real_block = np.where(column <= half, np.cos(angle), np.sin(angle)) * np.sqrt(weight)
    blocks = []
    for first in range(1, (ways + 1) // 2):
        angle = 2.0 * np.pi * (point * (first + ways * column) % length) / length
        cosine, sine = np.cos(angle), np.sin(angle)
        blocks.append(np.block([[cosine, -sine], [sine, cosine]]) / math.sqrt(LANES))
    return split_bf16_numpy(real_block), split_bf16_numpy(np.stack(blocks))


def dot_split(values, high_table, low_table, transposed):
    dims = (((1,), (1 if transposed else 0,)), ((), ()))
    high, low = split_bf16(values)
    dot = functools.partial(lax.dot_general, dimension_numbers=dims, preferred_element_type=jnp.float32)
    return dot(high, high_table) + (dot(low, high_table) + dot(high, low_table))


def damping_of(limit, wavenumber):
    ratio = limit / jnp.maximum(wavenumber, 1.0)
    return jnp.where(wavenumber > limit, ratio * ratio, 1.0)


def filter_kernel(sectors, cutoff_ref, *refs):
    circle_refs = refs[:sectors]
    real_high, real_low, block_high, block_low = refs[sectors:sectors + 4]
    own_out, first_out, second_out = refs[sectors + 4:sectors + 7]
    wide, real_wave, block_wave = refs[sectors + 7:]
    fields, levels, rows, sector = circle_refs[0].shape
    length = sector * sectors
    ways = length // LANES
    pairs = (ways - 1) // 2
    tiles = own_out.shape[-1] // LANES
    per_field = levels * rows
    lat = lax.axis_index("lat")
    limits = [cutoff_ref[lat * rows + j] for j in range(rows)]
    lowest = functools.reduce(jnp.minimum, limits)

    for k in range(sectors):
        wide[:, k * sector:(k + 1) * sector] = circle_refs[k][...].reshape(fields * per_field, sector)

    @pl.when(lowest < length // 2)
    def _():
        sublane = lax.broadcasted_iota(jnp.int32, (rows, LANES), 0)
        limit = jnp.zeros((rows, LANES), jnp.float32)
        for j in range(rows):
            limit = jnp.where(sublane == j, limits[j].astype(jnp.float32), limit)
        lane = lax.broadcasted_iota(jnp.int32, (rows, LANES), 1)

        def forward(field, carry):
            span = pl.ds(pl.multiple_of(field * per_field, per_field), per_field)
            tile = [wide[span, a * LANES:(a + 1) * LANES] for a in range(ways)]
            even = [tile[a] + tile[ways - a] for a in range(1, pairs + 1)]
            odd = [tile[a] - tile[ways - a] for a in range(1, pairs + 1)]
            real_wave[span, :] = tile[0] + sum(even)
            for k in range(1, pairs + 1):
                turn = [2.0 * math.pi * (a * k % ways) / ways for a in range(1, pairs + 1)]
                block_wave[k - 1, span, :LANES] = tile[0] + sum(math.cos(t) * e for t, e in zip(turn, even))
                block_wave[k - 1, span, LANES:] = -sum(math.sin(t) * o for t, o in zip(turn, odd))
            return carry

        lax.fori_loop(0, fields, forward, 0)

        def damp(spectrum, damping):
            shaped = spectrum.reshape(fields * levels, rows, damping.shape[-1])
            return (shaped * damping[None]).reshape(spectrum.shape)

        half = LANES // 2
        wave = (jnp.where(lane <= half, lane, lane - half) * ways).astype(jnp.float32)
        spectrum = dot_split(real_wave[...], real_high[...], real_low[...], False)
        spectrum = damp(spectrum, damping_of(limit, wave))
        real_wave[...] = dot_split(spectrum, real_high[...], real_low[...], True)
        for k in range(1, pairs + 1):
            mode = k + ways * lane
            one = damping_of(limit, jnp.minimum(mode, length - mode).astype(jnp.float32))
            damping = jnp.concatenate([one, one], axis=1)
            spectrum = dot_split(block_wave[k - 1], block_high[k - 1], block_low[k - 1], False)
            block_wave[k - 1] = dot_split(damp(spectrum, damping), block_high[k - 1], block_low[k - 1], True)

        def backward(field, carry):
            span = pl.ds(pl.multiple_of(field * per_field, per_field), per_field)
            base = real_wave[span, :] * (1.0 / ways)
            cosines = [block_wave[k, span, :LANES] for k in range(pairs)]
            sines = [block_wave[k, span, LANES:] for k in range(pairs)]
            wide[span, :LANES] = base + (2.0 / ways) * sum(cosines)
            for a in range(1, pairs + 1):
                turn = [2.0 * math.pi * (a * k % ways) / ways for k in range(1, pairs + 1)]
                even = base + sum((2.0 / ways * math.cos(t)) * c for t, c in zip(turn, cosines))
                odd = sum((2.0 / ways * math.sin(t)) * s for t, s in zip(turn, sines))
                wide[span, a * LANES:(a + 1) * LANES] = even - odd
                wide[span, (ways - a) * LANES:(ways - a + 1) * LANES] = even + odd
            return carry

        lax.fori_loop(0, fields, backward, 0)

    def emit(field, carry):
        span = pl.ds(pl.multiple_of(field * per_field, per_field), per_field)
        lane = lax.broadcasted_iota(jnp.int32, (per_field, LANES), 1)
        for a in range(tiles):
            tile = wide[span, a * LANES:(a + 1) * LANES]
            if a == tiles - 1:
                behind = wide[span, (ways - 1) * LANES:]
                tile = jnp.where(lane >= LANES - HALO, behind, tile)
            turned = jnp.swapaxes(tile.reshape(levels, rows, LANES), 0, 1)
            own_out[pl.ds(field, 1), :, :, a * LANES:(a + 1) * LANES] = turned[None]
        return carry

    lax.fori_loop(0, fields, emit, 0)
    top = rows - HALO
    to_next = lax.rem(lat, 2) == 0

    @pl.when(to_next)
    def _():
        first_out[...] = own_out[:, top:]
        second_out[...] = own_out[:, :HALO]

    @pl.when(jnp.logical_not(to_next))
    def _():
        first_out[...] = own_out[:, :HALO]
        second_out[...] = own_out[:, top:]


def rate_kernel(lat_ahead, lat_behind, lon_ahead, lon_behind, own_out, first_out, second_out):
    levels, rows, sector = lat_ahead.shape
    width = own_out.shape[-1]
    lat = lax.axis_index("lat")
    is_last = lat == lax.axis_size("lat") - 1
    for q, ref in enumerate((lat_ahead, lat_behind, lon_ahead, lon_behind)):
        for start in range(0, sector, LANES):
            stop = min(start + LANES, sector)
            tile = ref[:, :, start:stop]
            if stop - start < LANES:
                tile = jnp.pad(tile, ((0, 0), (0, 0), (0, LANES - (stop - start))))
            if q == 0:
                row = lax.broadcasted_iota(jnp.int32, tile.shape, 1)
                tile = jnp.where(jnp.logical_and(is_last, row == rows - 1), 0.0, tile)
            own_out[:, q, :, start:start + LANES] = jnp.swapaxes(tile, 0, 1)
    top = rows - HALO
    to_next = lax.rem(lat, 2) == 0

    @pl.when(to_next)
    def _():
        first_out[...] = own_out[top:]
        second_out[...] = own_out[:HALO]

    @pl.when(jnp.logical_not(to_next))
    def _():
        first_out[...] = own_out[:HALO]
        second_out[...] = own_out[top:]


def by_side(first_ref, second_ref, use):
    to_next = lax.rem(lax.axis_index("lat"), 2) == 0

    @pl.when(to_next)
    def _():
        use(second_ref, first_ref)

    @pl.when(jnp.logical_not(to_next))
    def _():
        use(first_ref, second_ref)


def rim_kernel(sector, own_ref, first_ref, second_ref, rim_out):
    rows = own_ref.shape[0]
    kinds = own_ref.shape[1]
    levels = own_ref.shape[2]
    edge = sector - HALO
    tile = edge // LANES * LANES
    lane = lax.broadcasted_iota(jnp.int32, (levels, LANES), 1)

    def rim_of(ref, count, base):
        def one(r, carry):
            packed = jnp.zeros((levels, LANES), jnp.float32)
            for q in range(kinds):
                at = 2 * HALO * q
                initial = pltpu.roll(ref[r, q, :, :LANES], at, 1) if at else ref[r, q, :, :LANES]
                shift = (at + HALO - (edge - tile)) % LANES
                last = pltpu.roll(ref[r, q, :, tile:tile + LANES], shift, 1)
                packed = jnp.where((lane >= at) & (lane < at + HALO), initial, packed)
                packed = jnp.where((lane >= at + HALO) & (lane < at + 2 * HALO), last, packed)
            rim_out[base + r] = packed
            return carry

        lax.fori_loop(0, count, one, 0)

    rim_of(own_ref, rows, HALO)

    def halos(below, above):
        rim_of(below, HALO, 0)
        rim_of(above, HALO, HALO + rows)

    by_side(first_ref, second_ref, halos)


def transport_kernel(chunks, sector, amplify, *refs):
    count = len(chunks)
    own_refs = refs[0:3 * count:3]
    first_refs = refs[1:3 * count:3]
    second_refs = refs[2:3 * count:3]
    rate_own, rate_first, rate_second, rim_ahead, rim_behind = refs[3 * count:3 * count + 5]
    out_ref = refs[3 * count + 5]
    current, coupled, rates = refs[3 * count + 6:]
    rows = own_refs[0].shape[1]
    levels, width = own_refs[0].shape[2:]
    fields = sum(chunks)
    kinds = 4
    extent = rows + 2 * HALO

    def load(below, above, own, field):
        def put(ref, base, number):
            def one(r, carry):
                current[base + r, field] = ref[r]
                return carry

            lax.fori_loop(0, number, one, 0)

        put(below, 0, HALO)
        put(own, HALO, rows)
        put(above, HALO + rows, HALO)

    field = 0
    for c in range(count):
        for j in range(chunks[c]):
            def use(below, above, c=c, j=j, field=field):
                load(below.at[j], above.at[j], own_refs[c].at[j], field)

            by_side(first_refs[c], second_refs[c], use)
            field += 1

    lane = lax.broadcasted_iota(jnp.int32, (levels, LANES), 1)
    ahead_tile, ahead_lane = sector // LANES, sector % LANES
    final = width // LANES - 1

    def extend(ref, count, base):
        def one(r, carry):
            ahead, behind = rim_ahead[base + r], rim_behind[base + r]
            for q in range(kinds):
                at = 2 * HALO * q
                for t in range(width // LANES):
                    piece = ref[r, q, :, t * LANES:(t + 1) * LANES]
                    if t == ahead_tile:
                        moved = pltpu.roll(ahead, (ahead_lane - at) % LANES, 1)
                        piece = jnp.where((lane >= ahead_lane) & (lane < ahead_lane + HALO), moved, piece)
                    if t == final:
                        moved = pltpu.roll(behind, (LANES - HALO - at - HALO) % LANES, 1)
                        piece = jnp.where(lane >= LANES - HALO, moved, piece)
                    if t >= ahead_tile:
                        inside = lane < sector + HALO - t * LANES
                        if t == final:
                            inside = inside | (lane >= LANES - HALO)
                        piece = jnp.where(inside, piece, 0.0)
                    rates[base + r, q, :, t * LANES:(t + 1) * LANES] = piece
            return carry

        lax.fori_loop(0, count, one, 0)

    extend(rate_own, rows, HALO)
    by_side(
        rate_first,
        rate_second,
        lambda below, above: (extend(below, HALO, 0), extend(above, HALO, HALO + rows)),
    )

    def combine(step, carry):
        r = extent - 2 - step
        south = rates[r - 1, 1]
        north = rates[r, 0]
        east = rates[r, 2]
        west = pltpu.roll(rates[r, 3], 1, 1)
        rates[r, 1] = south
        rates[r, 3] = west
        rates[r, 4] = 1.0 - east - west - north - south
        return carry

    lax.fori_loop(0, extent - 2, combine, 0)

    def couple(r):
        values = [current[r, g] for g in range(fields)]
        for f in range(fields):
            pieces = []
            for t in range(width // LANES):
                total = None
                for g in range(fields):
                    term = amplify[g, f] * values[g][:, t * LANES:(t + 1) * LANES]
                    total = term if total is None else total + term
                pieces.append(total)
            coupled[r, f] = jnp.concatenate(pieces, axis=1)

    def move(r):
        north, south, east, west, stay = (rates[r, q] for q in range(5))
        for f in range(fields):
            here = coupled[r, f]
            current[r, f] = (
                stay * here
                + east * pltpu.roll(here, width - 1, 1)
                + west * pltpu.roll(here, 1, 1)
                + north * coupled[r + 1, f]
                + south * coupled[r - 1, f]
            )

    def substep(step, carry):
        couple(step)
        couple(step + 1)

        def row(r, inner):
            couple(r + 1)
            move(r)
            return inner

        return lax.fori_loop(step + 1, extent - 1 - step, row, carry)

    lax.fori_loop(0, SUBSTEPS, substep, 0)

    for f in range(fields):
        for start in range(0, sector, LANES):
            stop = min(start + LANES, sector)
            tile = jnp.stack([current[HALO + r, f, :, start:start + LANES] for r in range(rows)])
            out_ref[f, :, :, start:stop] = jnp.swapaxes(tile, 0, 1)[:, :, :stop - start]


def lat_pairs(count):
    def both(start):
        ups = [(i, i + 1) for i in range(start, count - 1, 2)]
        return ups + [(j, i) for i, j in ups]

    return both(0), both(1)


def shards(adjoint_in, lat_ahead, lat_behind, lon_ahead, lon_behind, coupling, cutoff):
    fields, levels, rows, sector = adjoint_in.shape
    sectors = lax.axis_size("lon")
    length = sector * sectors
    width = -(-(sector + 2 * HALO) // LANES) * LANES
    even_pairs, odd_pairs = lat_pairs(lax.axis_size("lat"))
    f32 = jnp.float32
    chunks = CHUNKS if sum(CHUNKS) == fields else (fields,)

    def sector_ahead(values, offset):
        return lax.ppermute(values, "lon", [(s, (s - offset) % sectors) for s in range(sectors)])

    def to_bands(first, second):
        return lax.ppermute(first, "lat", even_pairs), lax.ppermute(second, "lat", odd_pairs)

    starts = [sum(chunks[:c]) for c in range(len(chunks))]
    parts = [adjoint_in[s:s + n] for s, n in zip(starts, chunks)]
    circles = [[part] + [sector_ahead(part, k) for k in range(1, sectors)] for part in parts]

    rate_shape = (4, levels, width)
    rate_own, rate_first, rate_second = pl.pallas_call(
        rate_kernel,
        out_shape=(
            jax.ShapeDtypeStruct((rows,) + rate_shape, f32),
            jax.ShapeDtypeStruct((HALO,) + rate_shape, f32),
            jax.ShapeDtypeStruct((HALO,) + rate_shape, f32),
        ),
        in_specs=[VMEM] * 4,
        out_specs=(VMEM,) * 3,
        name="rates",
    )(lat_ahead, lat_behind, lon_ahead, lon_behind)
    rate_first, rate_second = to_bands(rate_first, rate_second)
    rim = pl.pallas_call(
        functools.partial(rim_kernel, sector),
        out_shape=jax.ShapeDtypeStruct((rows + 2 * HALO, levels, LANES), f32),
        in_specs=[VMEM] * 3,
        out_specs=VMEM,
        name="rims",
    )(rate_own, rate_first, rate_second)
    rim_ahead = sector_ahead(rim, 1)
    rim_behind = rim_ahead if sectors == 2 else sector_ahead(rim, sectors - 1)

    (real_high, real_low), (block_high, block_low) = mode_tables(length)
    tables = [jnp.asarray(t) for t in (real_high, real_low, block_high, block_low)]
    moved = []
    for n, circle in zip(chunks, circles):
        lines = n * levels * rows
        own, first, second = pl.pallas_call(
            functools.partial(filter_kernel, sectors),
            out_shape=(
                jax.ShapeDtypeStruct((n, rows, levels, width), f32),
                jax.ShapeDtypeStruct((n, HALO, levels, width), f32),
                jax.ShapeDtypeStruct((n, HALO, levels, width), f32),
            ),
            in_specs=[SMEM] + [VMEM] * (sectors + 4),
            out_specs=(VMEM,) * 3,
            scratch_shapes=[
                pltpu.VMEM((lines, length), f32),
                pltpu.VMEM((lines, LANES), f32),
                pltpu.VMEM((block_high.shape[0], lines, 2 * LANES), f32),
            ],
            name="polar_filter",
        )(cutoff, *circle, *tables)
        moved += [own, *to_bands(first, second)]

    amplify = jnp.transpose(coupling + jnp.eye(fields, dtype=f32)[None], (1, 2, 0))
    amplify = jnp.broadcast_to(amplify[..., None], (fields, fields, levels, LANES))
    extent = rows + 2 * HALO
    return pl.pallas_call(
        functools.partial(transport_kernel, chunks, sector),
        out_shape=jax.ShapeDtypeStruct(adjoint_in.shape, f32),
        in_specs=[VMEM] * (1 + len(moved) + 5),
        out_specs=VMEM,
        scratch_shapes=[
            pltpu.VMEM((extent, fields, levels, width), f32),
            pltpu.VMEM((extent, fields, levels, width), f32),
            pltpu.VMEM((extent, 5, levels, width), f32),
        ],
        name="transport",
    )(amplify, *moved, rate_own, rate_first, rate_second, rim_ahead, rim_behind)


def solution(mesh):
    placed = (
        P("member", "lev", "lat", "lon"),
        P(("member", "lev"), "lat", "lon"),
        P(("member", "lev"), "lat", "lon"),
        P(("member", "lev"), "lat", "lon"),
        P(("member", "lev"), "lat", "lon"),
        P("lev", None, None),
        P(),
    )
    return jax.shard_map(
        shards,
        mesh=mesh,
        in_specs=placed,
        out_specs=P("member", "lev", "lat", "lon"),
        check_vma=False,
    )
```

```python
import functools
import math

import jax
import jax.numpy as jnp
import numpy as np
from jax import lax
from jax.experimental import pallas as pl
from jax.experimental.pallas import tpu as pltpu
from jax.sharding import PartitionSpec as P

SUBSTEPS = 6
HALO = SUBSTEPS
LANES = 128
CHUNKS = (2, 2, 1)
PARAMS = pltpu.CompilerParams(vmem_limit_bytes=12 * 2**20)
VMEM = pl.BlockSpec(memory_space=pltpu.VMEM)
SMEM = pl.BlockSpec(memory_space=pltpu.SMEM)


def split_bf16(values):
    high = values.astype(jnp.bfloat16)
    low = (values - high.astype(jnp.float32)).astype(jnp.bfloat16)
    return high, low


def split_bf16_numpy(values):
    values = values.astype(np.float32)
    high = values.astype(jnp.bfloat16)
    low = (values - high.astype(np.float32)).astype(jnp.bfloat16)
    return high, low


def mode_tables(length):
    ways = length // LANES
    point = np.arange(LANES)[:, None].astype(np.int64)
    column = np.arange(LANES)[None, :].astype(np.int64)
    half = LANES // 2
    wave = np.where(column <= half, column, column - half)
    angle = 2.0 * np.pi * (point * wave % LANES) / LANES
    weight = np.where((column == 0) | (column == half), 1.0 / LANES, 2.0 / LANES)
    real_block = np.where(column <= half, np.cos(angle), np.sin(angle)) * np.sqrt(weight)
    blocks = []
    for first in range(1, (ways + 1) // 2):
        angle = 2.0 * np.pi * (point * (first + ways * column) % length) / length
        cosine, sine = np.cos(angle), np.sin(angle)
        blocks.append(np.block([[cosine, -sine], [sine, cosine]]) / math.sqrt(LANES))
    return split_bf16_numpy(real_block), split_bf16_numpy(np.stack(blocks))


def dot_split(values, high_table, low_table, transposed):
    dims = (((1,), (1 if transposed else 0,)), ((), ()))
    count = values.shape[0]
    high, low = split_bf16(values)
    dot = functools.partial(lax.dot_general, dimension_numbers=dims, preferred_element_type=jnp.float32)
    main = dot(jnp.concatenate([high, low], axis=0), high_table)
    return main[:count] + (main[count:] + dot(high, low_table))


def damping_of(limit, wavenumber):
    ratio = limit / jnp.maximum(wavenumber, 1.0)
    return jnp.where(wavenumber > limit, ratio * ratio, 1.0)


def filter_kernel(sectors, cutoff_ref, *refs):
    circle_refs = refs[:sectors]
    real_high, real_low, block_high, block_low = refs[sectors:sectors + 4]
    own_out, first_out, second_out = refs[sectors + 4:sectors + 7]
    wide, real_wave, block_wave = refs[sectors + 7:]
    fields, levels, rows, sector = circle_refs[0].shape
    length = sector * sectors
    ways = length // LANES
    pairs = (ways - 1) // 2
    tiles = own_out.shape[-1] // LANES
    per_field = levels * rows
    lat = lax.axis_index("lat")
    limits = [cutoff_ref[lat * rows + j] for j in range(rows)]
    lowest = functools.reduce(jnp.minimum, limits)

    for k in range(sectors):
        wide[:, k * sector:(k + 1) * sector] = circle_refs[k][...].reshape(fields * per_field, sector)

    @pl.when(lowest < length // 2)
    def _():
        sublane = lax.broadcasted_iota(jnp.int32, (rows, LANES), 0)
        limit = jnp.zeros((rows, LANES), jnp.float32)
        for j in range(rows):
            limit = jnp.where(sublane == j, limits[j].astype(jnp.float32), limit)
        lane = lax.broadcasted_iota(jnp.int32, (rows, LANES), 1)

        def forward(field, carry):
            span = pl.ds(pl.multiple_of(field * per_field, per_field), per_field)
            tile = [wide[span, a * LANES:(a + 1) * LANES] for a in range(ways)]
            even = [tile[a] + tile[ways - a] for a in range(1, pairs + 1)]
            odd = [tile[a] - tile[ways - a] for a in range(1, pairs + 1)]
            real_wave[span, :] = tile[0] + sum(even)
            for k in range(1, pairs + 1):
                turn = [2.0 * math.pi * (a * k % ways) / ways for a in range(1, pairs + 1)]
                block_wave[k - 1, span, :LANES] = tile[0] + sum(math.cos(t) * e for t, e in zip(turn, even))
                block_wave[k - 1, span, LANES:] = -sum(math.sin(t) * o for t, o in zip(turn, odd))
            return carry

        lax.fori_loop(0, fields, forward, 0)

        def damp(spectrum, damping):
            shaped = spectrum.reshape(fields * levels, rows, damping.shape[-1])
            return (shaped * damping[None]).reshape(spectrum.shape)

        half = LANES // 2
        wave = (jnp.where(lane <= half, lane, lane - half) * ways).astype(jnp.float32)
        spectrum = dot_split(real_wave[...], real_high[...], real_low[...], False)
        spectrum = damp(spectrum, damping_of(limit, wave))
        real_wave[...] = dot_split(spectrum, real_high[...], real_low[...], True)
        for k in range(1, pairs + 1):
            mode = k + ways * lane
            one = damping_of(limit, jnp.minimum(mode, length - mode).astype(jnp.float32))
            damping = jnp.concatenate([one, one], axis=1)
            spectrum = dot_split(block_wave[k - 1], block_high[k - 1], block_low[k - 1], False)
            block_wave[k - 1] = dot_split(damp(spectrum, damping), block_high[k - 1], block_low[k - 1], True)

        def backward(field, carry):
            span = pl.ds(pl.multiple_of(field * per_field, per_field), per_field)
            base = real_wave[span, :] * (1.0 / ways)
            cosines = [block_wave[k, span, :LANES] for k in range(pairs)]
            sines = [block_wave[k, span, LANES:] for k in range(pairs)]
            wide[span, :LANES] = base + (2.0 / ways) * sum(cosines)
            for a in range(1, pairs + 1):
                turn = [2.0 * math.pi * (a * k % ways) / ways for k in range(1, pairs + 1)]
                even = base + sum((2.0 / ways * math.cos(t)) * c for t, c in zip(turn, cosines))
                odd = sum((2.0 / ways * math.sin(t)) * s for t, s in zip(turn, sines))
                wide[span, a * LANES:(a + 1) * LANES] = even - odd
                wide[span, (ways - a) * LANES:(ways - a + 1) * LANES] = even + odd
            return carry

        lax.fori_loop(0, fields, backward, 0)

    def emit(field, carry):
        span = pl.ds(pl.multiple_of(field * per_field, per_field), per_field)
        lane = lax.broadcasted_iota(jnp.int32, (per_field, LANES), 1)
        for a in range(tiles):
            tile = wide[span, a * LANES:(a + 1) * LANES]
            if a == tiles - 1:
                behind = wide[span, (ways - 1) * LANES:]
                tile = jnp.where(lane >= LANES - HALO, behind, tile)
            turned = jnp.swapaxes(tile.reshape(levels, rows, LANES), 0, 1)
            own_out[pl.ds(field, 1), :, :, a * LANES:(a + 1) * LANES] = turned[None]
        return carry

    lax.fori_loop(0, fields, emit, 0)
    top = rows - HALO
    to_next = lax.rem(lat, 2) == 0

    @pl.when(to_next)
    def _():
        first_out[...] = own_out[:, top:]
        second_out[...] = own_out[:, :HALO]

    @pl.when(jnp.logical_not(to_next))
    def _():
        first_out[...] = own_out[:, :HALO]
        second_out[...] = own_out[:, top:]


def rate_kernel(lat_ahead, lat_behind, lon_ahead, lon_behind, own_out, first_out, second_out):
    levels, rows, sector = lat_ahead.shape
    width = own_out.shape[-1]
    lat = lax.axis_index("lat")
    is_last = lat == lax.axis_size("lat") - 1
    for q, ref in enumerate((lat_ahead, lat_behind, lon_ahead, lon_behind)):
        for start in range(0, sector, LANES):
            stop = min(start + LANES, sector)
            tile = ref[:, :, start:stop]
            if stop - start < LANES:
                tile = jnp.pad(tile, ((0, 0), (0, 0), (0, LANES - (stop - start))))
            if q == 0:
                row = lax.broadcasted_iota(jnp.int32, tile.shape, 1)
                tile = jnp.where(jnp.logical_and(is_last, row == rows - 1), 0.0, tile)
            own_out[:, q, :, start:start + LANES] = jnp.swapaxes(tile, 0, 1)
    top = rows - HALO
    to_next = lax.rem(lat, 2) == 0

    @pl.when(to_next)
    def _():
        first_out[...] = own_out[top:]
        second_out[...] = own_out[:HALO]

    @pl.when(jnp.logical_not(to_next))
    def _():
        first_out[...] = own_out[:HALO]
        second_out[...] = own_out[top:]


def by_side(first_ref, second_ref, use):
    to_next = lax.rem(lax.axis_index("lat"), 2) == 0

    @pl.when(to_next)
    def _():
        use(second_ref, first_ref)

    @pl.when(jnp.logical_not(to_next))
    def _():
        use(first_ref, second_ref)


def coupling_power(coupling_ref):
    levels, fields, _ = coupling_ref.shape
    sublane = lax.broadcasted_iota(jnp.int32, (levels, LANES), 0)
    base = []
    for g in range(fields):
        base.append([])
        for f in range(fields):
            value = jnp.full((levels, LANES), coupling_ref[0, g, f], jnp.float32)
            for level in range(1, levels):
                value = jnp.where(sublane == level, coupling_ref[level, g, f], value)
            base[g].append(value + 1.0 if g == f else value)

    def product(left, right):
        def entry(g, f):
            return functools.reduce(jnp.add, [left[g][h] * right[h][f] for h in range(fields)])

        return [[entry(g, f) for f in range(fields)] for g in range(fields)]

    power = base
    for bit in bin(SUBSTEPS)[3:]:
        power = product(power, power)
        if bit == "1":
            power = product(power, base)
    return power


def rim_kernel(sector, coupling_ref, own_ref, first_ref, second_ref, rim_out, power_out):
    power = coupling_power(coupling_ref)
    for g, line in enumerate(power):
        for f, value in enumerate(line):
            power_out[g, f] = value
    rows = own_ref.shape[0]
    kinds = own_ref.shape[1]
    levels = own_ref.shape[2]
    edge = sector - HALO
    tile = edge // LANES * LANES
    lane = lax.broadcasted_iota(jnp.int32, (levels, LANES), 1)

    def rim_of(ref, count, base):
        def one(r, carry):
            packed = jnp.zeros((levels, LANES), jnp.float32)
            for q in range(kinds):
                at = 2 * HALO * q
                initial = pltpu.roll(ref[r, q, :, :LANES], at, 1) if at else ref[r, q, :, :LANES]
                shift = (at + HALO - (edge - tile)) % LANES
                last = pltpu.roll(ref[r, q, :, tile:tile + LANES], shift, 1)
                packed = jnp.where((lane >= at) & (lane < at + HALO), initial, packed)
                packed = jnp.where((lane >= at + HALO) & (lane < at + 2 * HALO), last, packed)
            rim_out[base + r] = packed
            return carry

        lax.fori_loop(0, count, one, 0)

    rim_of(own_ref, rows, HALO)

    def halos(below, above):
        rim_of(below, HALO, 0)
        rim_of(above, HALO, HALO + rows)

    by_side(first_ref, second_ref, halos)


def face_kernel(sector, rate_own, rate_first, rate_second, rim_ahead, rim_behind, rates):
    rows, kinds, levels, width = rate_own.shape
    extent = rows + 2 * HALO
    lane = lax.broadcasted_iota(jnp.int32, (levels, LANES), 1)
    ahead_tile, ahead_lane = sector // LANES, sector % LANES
    final = width // LANES - 1

    def extend(ref, count, base):
        def one(r, carry):
            ahead, behind = rim_ahead[base + r], rim_behind[base + r]
            for q in range(kinds):
                at = 2 * HALO * q
                for t in range(width // LANES):
                    piece = ref[r, q, :, t * LANES:(t + 1) * LANES]
                    if t == ahead_tile:
                        moved = pltpu.roll(ahead, (ahead_lane - at) % LANES, 1)
                        piece = jnp.where((lane >= ahead_lane) & (lane < ahead_lane + HALO), moved, piece)
                    if t == final:
                        moved = pltpu.roll(behind, (LANES - HALO - at - HALO) % LANES, 1)
                        piece = jnp.where(lane >= LANES - HALO, moved, piece)
                    if t >= ahead_tile:
                        inside = lane < sector + HALO - t * LANES
                        if t == final:
                            inside = inside | (lane >= LANES - HALO)
                        piece = jnp.where(inside, piece, 0.0)
                    rates[base + r, q, :, t * LANES:(t + 1) * LANES] = piece
            return carry

        lax.fori_loop(0, count, one, 0, unroll=2)

    extend(rate_own, rows, HALO)
    by_side(
        rate_first,
        rate_second,
        lambda below, above: (extend(below, HALO, 0), extend(above, HALO, HALO + rows)),
    )

    def combine(step, carry):
        r = extent - 2 - step
        here = [[rates[r - (q == 1), q, :, t * LANES:(t + 1) * LANES] for q in range(kinds)] for t in range(final + 1)]
        west = shifted([h[3] for h in here], 1)
        for t, (north, south, east, _) in enumerate(here):
            stay = 1.0 - east - west[t] - north - south
            for q, value in ((1, south), (3, west[t]), (4, stay)):
                rates[r, q, :, t * LANES:(t + 1) * LANES] = value
        return carry

    lax.fori_loop(0, extent - 2, combine, 0, unroll=2)


def shifted(tiles, step):
    lane = lax.broadcasted_iota(jnp.int32, tiles[0].shape, 1)
    rolled = [pltpu.roll(tile, step % LANES, 1) for tile in tiles]
    border = lane == (0 if step == 1 else LANES - 1)
    count = len(tiles)
    return [jnp.where(border, rolled[(t - step) % count], rolled[t]) for t in range(count)]


def transport_kernel(chunk, finished, sector, power_ref, rates, own_ref, first_ref, second_ref, *refs):
    earlier = refs[:finished]
    out_ref, even, odd = refs[finished:]
    rows, levels, width = own_ref.shape[1:]
    extent = rows + 2 * HALO
    tiles = width // LANES
    last = finished > 0

    def put(ref, base):
        even[:, base:base + ref.shape[1]] = ref[...]

    put(own_ref, HALO)

    def halos(below, above):
        put(below, 0)
        put(above, HALO + rows)

    by_side(first_ref, second_ref, halos)

    def line(source, r, field):
        return [source[field, r, :, t * LANES:(t + 1) * LANES] for t in range(tiles)]

    for step in range(SUBSTEPS):
        source, target = (even, odd) if step % 2 == 0 else (odd, even)

        def move(r):
            for field in range(chunk):
                here = line(source, r, field)
                above, below = line(source, r + 1, field), line(source, r - 1, field)
                ahead, behind = shifted(here, -1), shifted(here, 1)
                for t in range(tiles):
                    north, south, east, west, stay = (
                        rates[r, q, :, t * LANES:(t + 1) * LANES] for q in range(5)
                    )
                    target[field, r, :, t * LANES:(t + 1) * LANES] = (
                        stay * here[t]
                        + east * ahead[t]
                        + west * behind[t]
                        + north * above[t]
                        + south * below[t]
                    )

        def two_rows(pair, carry, step=step, move=move):
            move(step + 1 + 2 * pair)
            move(step + 2 + 2 * pair)
            return carry

        count = extent - 2 - 2 * step
        lax.fori_loop(0, count // 2, two_rows, 0)
        if count % 2:
            move(extent - 2 - step)
    result = even if SUBSTEPS % 2 == 0 else odd

    if not last:
        out_ref[...] = result[:, HALO:HALO + rows]
        return
    sources = [(ref, j, 0) for ref in earlier for j in range(ref.shape[0])]
    sources += [(result, j, HALO) for j in range(chunk)]
    fields = len(sources)
    for start in range(0, sector, LANES):
        stop = min(start + LANES, sector)
        values = [ref[j, base:base + rows, :, start:start + LANES] for ref, j, base in sources]
        for f in range(fields):
            total = functools.reduce(jnp.add, [power_ref[g, f][None] * values[g] for g in range(fields)])
            out_ref[f, :, :, start:stop] = jnp.swapaxes(total, 0, 1)[:, :, :stop - start]


def lat_pairs(count):
    def both(start):
        ups = [(i, i + 1) for i in range(start, count - 1, 2)]
        return ups + [(j, i) for i, j in ups]

    return both(0), both(1)


def shards(adjoint_in, lat_ahead, lat_behind, lon_ahead, lon_behind, coupling, cutoff):
    fields, levels, rows, sector = adjoint_in.shape
    sectors = lax.axis_size("lon")
    length = sector * sectors
    width = -(-(sector + 2 * HALO) // LANES) * LANES
    even_pairs, odd_pairs = lat_pairs(lax.axis_size("lat"))
    f32 = jnp.float32
    chunks = CHUNKS if sum(CHUNKS) == fields else (fields,)

    def sector_ahead(values, offset):
        return lax.ppermute(values, "lon", [(s, (s - offset) % sectors) for s in range(sectors)])

    def to_bands(first, second):
        return lax.ppermute(first, "lat", even_pairs), lax.ppermute(second, "lat", odd_pairs)

    starts = [sum(chunks[:c]) for c in range(len(chunks))]
    parts = [adjoint_in[s:s + n] for s, n in zip(starts, chunks)]
    circles = [[part] + [sector_ahead(part, k) for k in range(1, sectors)] for part in parts]

    rate_shape = (4, levels, width)
    rate_own, rate_first, rate_second = pl.pallas_call(
        rate_kernel,
        out_shape=(
            jax.ShapeDtypeStruct((rows,) + rate_shape, f32),
            jax.ShapeDtypeStruct((HALO,) + rate_shape, f32),
            jax.ShapeDtypeStruct((HALO,) + rate_shape, f32),
        ),
        in_specs=[VMEM] * 4,
        out_specs=(VMEM,) * 3,
        compiler_params=PARAMS,
        name="rates",
    )(lat_ahead, lat_behind, lon_ahead, lon_behind)
    rate_first, rate_second = to_bands(rate_first, rate_second)
    rim, power = pl.pallas_call(
        functools.partial(rim_kernel, sector),
        out_shape=(
            jax.ShapeDtypeStruct((rows + 2 * HALO, levels, LANES), f32),
            jax.ShapeDtypeStruct((fields, fields, levels, LANES), f32),
        ),
        in_specs=[SMEM] + [VMEM] * 3,
        out_specs=(VMEM,) * 2,
        compiler_params=PARAMS,
        name="rims",
    )(coupling, rate_own, rate_first, rate_second)
    rim_ahead = sector_ahead(rim, 1)
    rim_behind = rim_ahead if sectors == 2 else sector_ahead(rim, sectors - 1)

    extent = rows + 2 * HALO
    rates = pl.pallas_call(
        functools.partial(face_kernel, sector),
        out_shape=jax.ShapeDtypeStruct((extent, 5, levels, width), f32),
        in_specs=[VMEM] * 5,
        out_specs=VMEM,
        compiler_params=PARAMS,
        name="faces",
    )(rate_own, rate_first, rate_second, rim_ahead, rim_behind)

    (real_high, real_low), (block_high, block_low) = mode_tables(length)
    tables = [jnp.asarray(t) for t in (real_high, real_low, block_high, block_low)]
    results = []
    for c, (n, circle) in enumerate(zip(chunks, circles)):
        lines = n * levels * rows
        own, first, second = pl.pallas_call(
            functools.partial(filter_kernel, sectors),
            out_shape=(
                jax.ShapeDtypeStruct((n, rows, levels, width), f32),
                jax.ShapeDtypeStruct((n, HALO, levels, width), f32),
                jax.ShapeDtypeStruct((n, HALO, levels, width), f32),
            ),
            in_specs=[SMEM] + [VMEM] * (sectors + 4),
            out_specs=(VMEM,) * 3,
            scratch_shapes=[
                pltpu.VMEM((lines, length), f32),
                pltpu.VMEM((lines, LANES), f32),
                pltpu.VMEM((block_high.shape[0], lines, 2 * LANES), f32),
            ],
            compiler_params=PARAMS,
            name="polar_filter",
        )(cutoff, *circle, *tables)
        first, second = to_bands(first, second)
        is_last = c == len(chunks) - 1
        earlier = results if is_last else []
        shape = adjoint_in.shape if is_last else (n, rows, levels, width)
        results.append(pl.pallas_call(
            functools.partial(transport_kernel, n, len(earlier), sector),
            out_shape=jax.ShapeDtypeStruct(shape, f32),
            in_specs=[VMEM] * (5 + len(earlier)),
            out_specs=VMEM,
            scratch_shapes=[
                pltpu.VMEM((n, extent, levels, width), f32),
                pltpu.VMEM((n, extent, levels, width), f32),
            ],
            compiler_params=PARAMS,
            name="transport",
        )(power, rates, own, first, second, *earlier))
    return results[-1]


def solution(mesh):
    placed = (
        P("member", "lev", "lat", "lon"),
        P(("member", "lev"), "lat", "lon"),
        P(("member", "lev"), "lat", "lon"),
        P(("member", "lev"), "lat", "lon"),
        P(("member", "lev"), "lat", "lon"),
        P("lev", None, None),
        P(),
    )
    return jax.shard_map(
        shards,
        mesh=mesh,
        in_specs=placed,
        out_specs=P("member", "lev", "lat", "lon"),
        check_vma=False,
    )
```

```python
import functools
import math

import jax
import jax.numpy as jnp
import numpy as np
from jax import lax
from jax.experimental import pallas as pl
from jax.experimental.pallas import tpu as pltpu
from jax.sharding import PartitionSpec as P

SUBSTEPS = 6
HALO = SUBSTEPS
LANES = 128
RATES = 4
CHUNKS = (3, 2)
ROWS_AT_ONCE = 2
PARAMS = pltpu.CompilerParams(vmem_limit_bytes=12 * 2**20)
VMEM = pl.BlockSpec(memory_space=pltpu.VMEM)
HBM = pl.BlockSpec(memory_space=pltpu.HBM)


def split_bf16(values):
    high = values.astype(jnp.bfloat16)
    low = (values - high.astype(jnp.float32)).astype(jnp.bfloat16)
    return high, low


def split_bf16_numpy(values):
    values = values.astype(np.float32)
    high = values.astype(jnp.bfloat16)
    low = (values - high.astype(np.float32)).astype(jnp.bfloat16)
    return high, low


def mode_tables(length):
    ways = length // LANES
    point = np.arange(LANES)[:, None].astype(np.int64)
    column = np.arange(LANES)[None, :].astype(np.int64)
    half = LANES // 2
    wave = np.where(column <= half, column, column - half)
    angle = 2.0 * np.pi * (point * wave % LANES) / LANES
    weight = np.where((column == 0) | (column == half), 1.0 / LANES, 2.0 / LANES)
    real_block = np.where(column <= half, np.cos(angle), np.sin(angle)) * np.sqrt(weight)
    blocks = []
    for first in range(1, (ways + 1) // 2):
        angle = 2.0 * np.pi * (point * (first + ways * column) % length) / length
        cosine, sine = np.cos(angle), np.sin(angle)
        blocks.append(np.block([[cosine, -sine], [sine, cosine]]) / math.sqrt(LANES))
    block_high, block_low = split_bf16_numpy(np.stack(blocks))
    real = np.zeros((1, 2 * LANES, 2 * LANES), block_high.dtype)
    real[0, :LANES, :LANES], real[0, :LANES, LANES:] = split_bf16_numpy(real_block)
    return np.concatenate([block_high, block_low, real])


def dot_split(values, high_table, low_table, transposed):
    dims = (((1,), (1 if transposed else 0,)), ((), ()))
    count = values.shape[0]
    high, low = split_bf16(values)
    dot = functools.partial(lax.dot_general, dimension_numbers=dims, preferred_element_type=jnp.float32)
    main = dot(jnp.concatenate([high, low], axis=0), high_table)
    return main[:count] + (main[count:] + dot(high, low_table))


def damping_of(limit, wavenumber):
    ratio = limit / jnp.maximum(wavenumber, 1.0)
    return jnp.where(wavenumber > limit, ratio * ratio, 1.0)


def filter_kernel(sectors, edges, limit_ref, table, *refs):
    circle_refs = refs[:sectors]
    own_out, first_out, second_out = refs[sectors:sectors + 3]
    wide, real_wave, block_wave = refs[sectors + 3:]
    fields, levels, rows, width = circle_refs[0].shape
    sector = wide.shape[1] // sectors
    length = sector * sectors
    ways = length // LANES
    pairs = (ways - 1) // 2
    tiles = width // LANES
    per_field = levels * rows
    lat = lax.axis_index("lat")
    limit = limit_ref[...]

    for k in range(sectors):
        wide[:, k * sector:(k + 1) * sector] = circle_refs[k][:, :, :, :sector].reshape(fields * per_field, sector)

    @pl.when(jnp.min(limit) < length // 2)
    def _():
        lane = lax.broadcasted_iota(jnp.int32, (rows, LANES), 1)

        def forward(field, carry):
            span = pl.ds(pl.multiple_of(field * per_field, per_field), per_field)
            tile = [wide[span, a * LANES:(a + 1) * LANES] for a in range(ways)]
            even = [tile[a] + tile[ways - a] for a in range(1, pairs + 1)]
            odd = [tile[a] - tile[ways - a] for a in range(1, pairs + 1)]
            real_wave[span, :] = tile[0] + sum(even)
            for k in range(1, pairs + 1):
                turn = [2.0 * math.pi * (a * k % ways) / ways for a in range(1, pairs + 1)]
                block_wave[k - 1, span, :LANES] = tile[0] + sum(math.cos(t) * e for t, e in zip(turn, even))
                block_wave[k - 1, span, LANES:] = -sum(math.sin(t) * o for t, o in zip(turn, odd))
            return carry

        lax.fori_loop(0, fields, forward, 0)

        def damp(spectrum, damping):
            shaped = spectrum.reshape(fields * levels, rows, damping.shape[-1])
            return (shaped * damping[None]).reshape(spectrum.shape)

        half = LANES // 2
        wave = (jnp.where(lane <= half, lane, lane - half) * ways).astype(jnp.float32)
        real_high, real_low = table[2 * pairs, :LANES, :LANES], table[2 * pairs, :LANES, LANES:]
        spectrum = dot_split(real_wave[...], real_high, real_low, False)
        spectrum = damp(spectrum, damping_of(limit, wave))
        real_wave[...] = dot_split(spectrum, real_high, real_low, True)
        for k in range(1, pairs + 1):
            mode = k + ways * lane
            one = damping_of(limit, jnp.minimum(mode, length - mode).astype(jnp.float32))
            damping = jnp.concatenate([one, one], axis=1)
            high, low = table[k - 1], table[pairs + k - 1]
            spectrum = dot_split(block_wave[k - 1], high, low, False)
            block_wave[k - 1] = dot_split(damp(spectrum, damping), high, low, True)

        def backward(field, carry):
            span = pl.ds(pl.multiple_of(field * per_field, per_field), per_field)
            base = real_wave[span, :] * (1.0 / ways)
            cosines = [block_wave[k, span, :LANES] for k in range(pairs)]
            sines = [block_wave[k, span, LANES:] for k in range(pairs)]
            wide[span, :LANES] = base + (2.0 / ways) * sum(cosines)
            for a in range(1, pairs + 1):
                turn = [2.0 * math.pi * (a * k % ways) / ways for k in range(1, pairs + 1)]
                even = base + sum((2.0 / ways * math.cos(t)) * c for t, c in zip(turn, cosines))
                odd = sum((2.0 / ways * math.sin(t)) * s for t, s in zip(turn, sines))
                wide[span, a * LANES:(a + 1) * LANES] = even - odd
                wide[span, (ways - a) * LANES:(ways - a + 1) * LANES] = even + odd
            return carry

        lax.fori_loop(0, fields, backward, 0)

    def emit(field, carry):
        span = pl.ds(pl.multiple_of(field * per_field, per_field), per_field)
        lane = lax.broadcasted_iota(jnp.int32, (per_field, LANES), 1)
        for a in range(tiles):
            tile = wide[span, a * LANES:(a + 1) * LANES]
            if a == tiles - 1:
                behind = wide[span, (ways - 1) * LANES:]
                tile = jnp.where(lane >= LANES - HALO, behind, tile)
            turned = jnp.swapaxes(tile.reshape(levels, rows, LANES), 0, 1)
            own_out[pl.ds(field, 1), :, :, a * LANES:(a + 1) * LANES] = turned[None]
        return carry

    lax.fori_loop(0, fields, emit, 0)
    if edges:
        final = slice(width - LANES, width)
        ahead = jnp.swapaxes(circle_refs[1][0, :, :, final], 0, 1)
        behind = jnp.swapaxes(circle_refs[sectors - 1][0, :, :, final], 0, 1)
        first_lane = edge_lane(sector)
        lane = lax.broadcasted_iota(jnp.int32, (rows, levels, LANES), 2) - first_lane
        spare = jnp.where(lane % (2 * HALO) < HALO, ahead, behind)
        spare = jnp.where((lane >= 0) & (lane < RATES * 2 * HALO), spare, own_out[0, :, :, final])
        own_out[0, :, :, final] = spare

    top = rows - HALO
    to_next = lax.rem(lat, 2) == 0

    @pl.when(to_next)
    def _():
        first_out[...] = own_out[:, top:]
        second_out[...] = own_out[:, :HALO]

    @pl.when(jnp.logical_not(to_next))
    def _():
        first_out[...] = own_out[:, :HALO]
        second_out[...] = own_out[:, top:]


def edge_lane(sector):
    return sector % LANES + HALO


def limits_of(cutoff, rows):
    lat = lax.axis_index("lat")
    own = lax.dynamic_slice_in_dim(cutoff, lat * rows, rows, 0).astype(jnp.float32)
    return jnp.broadcast_to(own[:, None], (rows, LANES))


def pack_kernel(chunks, adjoint, *refs):
    sources = (adjoint,) + refs[:RATES]
    count = len(chunks)
    payloads = refs[RATES:RATES + count]
    own_out, first_out, second_out = refs[RATES + count:RATES + count + 3]
    state, rates, sems = refs[RATES + count + 3:]
    levels, rows, sector = sources[1].shape
    width = own_out.shape[-1]
    final = slice(width - LANES, width)
    tail = sector - (width - LANES)
    copies = [pltpu.make_async_copy(src, rates.at[q], sems.at[q]) for q, src in enumerate(sources[1:])]
    copies.append(pltpu.make_async_copy(adjoint, state, sems.at[RATES]))
    for copy in copies:
        copy.start()
    for copy in copies[:RATES]:
        copy.wait()
    lat = lax.axis_index("lat")
    is_last = lat == lax.axis_size("lat") - 1
    lane = lax.broadcasted_iota(jnp.int32, (levels, rows, LANES), 2)
    row = lax.broadcasted_iota(jnp.int32, (levels, rows, LANES), 1)
    edges = jnp.zeros((levels, rows, LANES), jnp.float32)
    for q in range(RATES):
        at = edge_lane(sector) + 2 * HALO * q
        for start in range(0, width, LANES):
            size = min(LANES, sector - start)
            tile = rates[q, :, :, start:start + size]
            if size < LANES:
                tile = jnp.concatenate([tile, jnp.zeros((levels, rows, LANES - size), jnp.float32)], axis=2)
            if q == 0:
                tile = jnp.where(jnp.logical_and(is_last, row == rows - 1), 0.0, tile)
            own_out[:, q, :, start:start + LANES] = jnp.swapaxes(tile, 0, 1)
            if start == 0:
                initial = pltpu.roll(tile, at, 2)
                edges = jnp.where((lane >= at) & (lane < at + HALO), initial, edges)
            if start == width - LANES:
                last = pltpu.roll(tile, (at + HALO - (tail - HALO)) % LANES, 2)
                edges = jnp.where((lane >= at + HALO) & (lane < at + 2 * HALO), last, edges)
    copies[RATES].wait()
    field = 0
    for c in range(count):
        for j in range(chunks[c]):
            payloads[c][j, :, :, :width - LANES] = state[field, :, :, :width - LANES]
            end = state[field, :, :, width - LANES:]
            end = jnp.concatenate([end, jnp.zeros((levels, rows, LANES - tail), jnp.float32)], axis=2)
            if field == 0:
                end = jnp.where(lane < tail, end, edges)
            payloads[c][j, :, :, final] = end
            field += 1
    top = rows - HALO
    to_next = lax.rem(lat, 2) == 0

    @pl.when(to_next)
    def _():
        first_out[...] = own_out[top:]
        second_out[...] = own_out[:HALO]

    @pl.when(jnp.logical_not(to_next))
    def _():
        first_out[...] = own_out[:HALO]
        second_out[...] = own_out[top:]


def by_side(first_ref, second_ref, use):
    to_next = lax.rem(lax.axis_index("lat"), 2) == 0

    @pl.when(to_next)
    def _():
        use(second_ref, first_ref)

    @pl.when(jnp.logical_not(to_next))
    def _():
        use(first_ref, second_ref)


def coupling_power(coupling_ref):
    fields, levels, _ = coupling_ref.shape
    base = []
    for g in range(fields):
        line = coupling_ref[g]
        base.append([jnp.broadcast_to(line[:, f:f + 1], (levels, LANES)) for f in range(fields)])
        base[g][g] = base[g][g] + 1.0

    def product(left, right):
        def entry(g, f):
            return functools.reduce(jnp.add, [left[g][h] * right[h][f] for h in range(fields)])

        return [[entry(g, f) for f in range(fields)] for g in range(fields)]

    power = base
    for bit in bin(SUBSTEPS)[3:]:
        power = product(power, power)
        if bit == "1":
            power = product(power, base)
    return power


def face_kernel(sector, coupling, rate_own, rate_first, rate_second, own, first, second, level, moved, power_out):
    power = coupling_power(coupling)
    for g, entries in enumerate(power):
        for f, value in enumerate(entries):
            power_out[g, f] = value
    rows, kinds, levels, width = rate_own.shape
    extent = rows + 2 * HALO
    tiles = width // LANES
    final = slice(width - LANES, width)
    lane = lax.broadcasted_iota(jnp.int32, (levels, LANES), 1)
    end = sector % LANES

    def extend(ref, edge_ref, base):
        count = ref.shape[0]
        for q in range(kinds):
            at = edge_lane(sector) + 2 * HALO * q
            edges = [edge_ref[0, r, :, final] for r in range(count)]
            ahead = [pltpu.roll(e, (end - at) % LANES, 1) for e in edges]
            behind = [pltpu.roll(e, (LANES - HALO - at - HALO) % LANES, 1) for e in edges]
            for r in range(count):
                piece = jnp.where((lane >= end) & (lane < end + HALO), ahead[r], ref[r, q, :, final])
                piece = jnp.where(lane >= LANES - HALO, behind[r], piece)
                level[base + r, q, :, :width - LANES] = ref[r, q, :, :width - LANES]
                level[base + r, q, :, final] = piece

    extend(rate_own, own, HALO)

    def halos(below, above, below_edges, above_edges):
        extend(below, below_edges, 0)
        extend(above, above_edges, HALO + rows)

    to_next = lax.rem(lax.axis_index("lat"), 2) == 0

    @pl.when(to_next)
    def _():
        halos(rate_second, rate_first, second, first)

    @pl.when(jnp.logical_not(to_next))
    def _():
        halos(rate_first, rate_second, first, second)

    def combine(step, carry):
        r = extent - 2 - step

        def tiles_of(index, q):
            return [level[index, q, :, t * LANES:(t + 1) * LANES] for t in range(tiles)]

        north, south, east, behind = tiles_of(r, 0), tiles_of(r - 1, 1), tiles_of(r, 2), tiles_of(r, 3)
        west = shifted(behind, 1)
        north_moved, south_moved, east_moved = shifted(north, -1), shifted(south, -1), shifted(east, -1)
        for t in range(tiles):
            span = slice(t * LANES, (t + 1) * LANES)
            level[r, 1, :, span] = south[t]
            level[r, 3, :, span] = west[t]
            level[r, 4, :, span] = 1.0 - east[t] - west[t] - north[t] - south[t]
            moved[r, 0, :, span] = north_moved[t]
            moved[r, 1, :, span] = south_moved[t]
            moved[r, 2, :, span] = east_moved[t]
            moved[r, 3, :, span] = behind[t]
            moved[r, 4, :, span] = 1.0 - east_moved[t] - behind[t] - north_moved[t] - south_moved[t]
        return carry

    lax.fori_loop(0, extent - 2, combine, 0)


def shifted(tiles, step):
    lane = lax.broadcasted_iota(jnp.int32, tiles[0].shape, 1)
    rolled = [pltpu.roll(tile, step % LANES, 1) for tile in tiles]
    border = lane == (0 if step == 1 else LANES - 1)
    count = len(tiles)
    return [jnp.where(border, rolled[(t - step) % count], rolled[t]) for t in range(count)]


def transport_kernel(chunk, finished, sector, power_ref, level, moved, own_ref, first_ref, second_ref, *refs):
    earlier = refs[:finished]
    out_ref, even, odd = refs[finished:]
    rows, levels, width = own_ref.shape[1:]
    extent = rows + 2 * HALO
    tiles = width // LANES
    last = finished > 0

    def put(ref, base):
        even[:, base:base + ref.shape[1]] = ref[...]

    put(own_ref, HALO)

    def halos(below, above):
        put(below, 0)
        put(above, HALO + rows)

    by_side(first_ref, second_ref, halos)

    def line(source, r, field):
        return [source[field, r, :, t * LANES:(t + 1) * LANES] for t in range(tiles)]

    for step in range(SUBSTEPS):
        forward = step % 2 == 0
        source, target, rates, way = (even, odd, moved, -1) if forward else (odd, even, level, 1)

        def move(r, field, below, here, above, twice):
            for t in range(tiles):
                span = slice(t * LANES, (t + 1) * LANES)
                north, south, east, west, stay = (rates[r, q, :, span] for q in range(5))
                plain = source[field, r, :, span]
                ahead, behind = (twice[t], plain) if forward else (plain, twice[t])
                target[field, r, :, span] = (
                    (stay * here[t] + (north * above[t] + south * below[t]))
                    + (east * ahead + west * behind)
                )

        for field in range(chunk):
            def turn(r):
                return shifted(line(source, r, field), way)

            def some_rows(index, carry):
                r = step + 1 + ROWS_AT_ONCE * index
                below, here = carry[:tiles], carry[tiles:]
                for j in range(ROWS_AT_ONCE):
                    above = turn(r + j + 1)
                    move(r + j, field, below, here, above, shifted(here, way))
                    below, here = here, above
                return tuple(below) + tuple(here)

            count = extent - 2 - 2 * step
            start = tuple(turn(step)) + tuple(turn(step + 1))
            lax.fori_loop(0, count // ROWS_AT_ONCE, some_rows, start, unroll=2)
    result = even if SUBSTEPS % 2 == 0 else odd

    if not last:
        out_ref[...] = result[:, HALO:HALO + rows]
        return
    sources = [(ref, j, 0) for ref in earlier for j in range(ref.shape[0])]
    sources += [(result, j, HALO) for j in range(chunk)]
    fields = len(sources)
    for start in range(0, sector, LANES):
        stop = min(start + LANES, sector)
        values = [ref[j, base:base + rows, :, start:start + LANES] for ref, j, base in sources]
        for f in range(fields):
            total = functools.reduce(jnp.add, [power_ref[g, f][None] * values[g] for g in range(fields)])
            out_ref[f, :, :, start:stop] = jnp.swapaxes(total, 0, 1)[:, :, :stop - start]


def lat_pairs(count):
    def both(start):
        ups = [(i, i + 1) for i in range(start, count - 1, 2)]
        return ups + [(j, i) for i, j in ups]

    return both(0), both(1)


def shards(adjoint_in, lat_ahead, lat_behind, lon_ahead, lon_behind, coupling, cutoff):
    fields, levels, rows, sector = adjoint_in.shape
    sectors = lax.axis_size("lon")
    length = sector * sectors
    width = -(-(sector + 2 * HALO) // LANES) * LANES
    even_pairs, odd_pairs = lat_pairs(lax.axis_size("lat"))
    f32 = jnp.float32
    chunks = CHUNKS if sum(CHUNKS) == fields else (fields,)

    def sector_ahead(values, offset):
        return lax.ppermute(values, "lon", [(s, (s - offset) % sectors) for s in range(sectors)])

    def to_bands(first, second):
        return lax.ppermute(first, "lat", even_pairs), lax.ppermute(second, "lat", odd_pairs)

    extent = rows + 2 * HALO
    rate_shape = (RATES, levels, width)
    *payloads, rate_own, rate_first, rate_second = pl.pallas_call(
        functools.partial(pack_kernel, chunks),
        out_shape=(
            *(jax.ShapeDtypeStruct((n, levels, rows, width), f32) for n in chunks),
            jax.ShapeDtypeStruct((rows,) + rate_shape, f32),
            jax.ShapeDtypeStruct((HALO,) + rate_shape, f32),
            jax.ShapeDtypeStruct((HALO,) + rate_shape, f32),
        ),
        in_specs=[HBM] * (1 + RATES),
        out_specs=(VMEM,) * (len(chunks) + 3),
        scratch_shapes=[
            pltpu.VMEM(adjoint_in.shape, f32),
            pltpu.VMEM((RATES,) + lat_ahead.shape, f32),
            pltpu.SemaphoreType.DMA((1 + RATES,)),
        ],
        compiler_params=PARAMS,
        name="pack",
    )(adjoint_in, lat_ahead, lat_behind, lon_ahead, lon_behind)
    circles = [[part] + [sector_ahead(part, k) for k in range(1, sectors)] for part in payloads]
    rate_first, rate_second = to_bands(rate_first, rate_second)

    limits = limits_of(cutoff, rows)
    table = jnp.asarray(mode_tables(length))
    results = []
    for c, (n, circle) in enumerate(zip(chunks, circles)):
        lines = n * levels * rows
        own, first, second = pl.pallas_call(
            functools.partial(filter_kernel, sectors, c == 0),
            out_shape=(
                jax.ShapeDtypeStruct((n, rows, levels, width), f32),
                jax.ShapeDtypeStruct((n, HALO, levels, width), f32),
                jax.ShapeDtypeStruct((n, HALO, levels, width), f32),
            ),
            in_specs=[VMEM] * (sectors + 2),
            out_specs=(VMEM,) * 3,
            scratch_shapes=[
                pltpu.VMEM((lines, length), f32),
                pltpu.VMEM((lines, LANES), f32),
                pltpu.VMEM((table.shape[0] // 2, lines, 2 * LANES), f32),
            ],
            compiler_params=PARAMS,
            name="polar_filter",
        )(limits, table, *circle)
        first, second = to_bands(first, second)
        if c == 0:
            level, moved, power = pl.pallas_call(
                functools.partial(face_kernel, sector),
                out_shape=(
                    jax.ShapeDtypeStruct((extent, 5, levels, width), f32),
                    jax.ShapeDtypeStruct((extent, 5, levels, width), f32),
                    jax.ShapeDtypeStruct((fields, fields, levels, LANES), f32),
                ),
                in_specs=[VMEM] * 7,
                out_specs=(VMEM,) * 3,
                compiler_params=PARAMS,
                name="faces",
            )(jnp.transpose(coupling, (1, 0, 2)), rate_own, rate_first, rate_second, own, first, second)
        is_last = c == len(chunks) - 1
        earlier = results if is_last else []
        shape = adjoint_in.shape if is_last else (n, rows, levels, width)
        results.append(pl.pallas_call(
            functools.partial(transport_kernel, n, len(earlier), sector),
            out_shape=jax.ShapeDtypeStruct(shape, f32),
            in_specs=[VMEM] * (6 + len(earlier)),
            out_specs=VMEM,
            scratch_shapes=[
                pltpu.VMEM((n, extent, levels, width), f32),
                pltpu.VMEM((n, extent, levels, width), f32),
            ],
            compiler_params=PARAMS,
            name="transport",
        )(power, level, moved, own, first, second, *earlier))
    return results[-1]


def solution(mesh):
    placed = (
        P("member", "lev", "lat", "lon"),
        P(("member", "lev"), "lat", "lon"),
        P(("member", "lev"), "lat", "lon"),
        P(("member", "lev"), "lat", "lon"),
        P(("member", "lev"), "lat", "lon"),
        P("lev", None, None),
        P(),
    )
    return jax.shard_map(
        shards,
        mesh=mesh,
        in_specs=placed,
        out_specs=P("member", "lev", "lat", "lon"),
        check_vma=False,
    )
```

```python
import functools
import math

import jax
import jax.numpy as jnp
import numpy as np
from jax import lax
from jax.experimental import pallas as pl
from jax.experimental.pallas import tpu as pltpu
from jax.sharding import PartitionSpec as P

SUBSTEPS = 6
HALO = SUBSTEPS
LANES = 128
RATES = 4
CHUNKS = (3, 2)
ROWS_AT_ONCE = 9
PARAMS = pltpu.CompilerParams(vmem_limit_bytes=12 * 2**20)
VMEM = pl.BlockSpec(memory_space=pltpu.VMEM)
HBM = pl.BlockSpec(memory_space=pltpu.HBM)


def split_bf16(values):
    high = values.astype(jnp.bfloat16)
    low = (values - high.astype(jnp.float32)).astype(jnp.bfloat16)
    return high, low


def split_bf16_numpy(values):
    values = values.astype(np.float32)
    high = values.astype(jnp.bfloat16)
    low = (values - high.astype(np.float32)).astype(jnp.bfloat16)
    return high, low


def mode_tables(length):
    ways = length // LANES
    point = np.arange(LANES)[:, None].astype(np.int64)
    column = np.arange(LANES)[None, :].astype(np.int64)
    half = LANES // 2
    wave = np.where(column <= half, column, column - half)
    angle = 2.0 * np.pi * (point * wave % LANES) / LANES
    weight = np.where((column == 0) | (column == half), 1.0 / LANES, 2.0 / LANES)
    real_block = np.where(column <= half, np.cos(angle), np.sin(angle)) * np.sqrt(weight)
    blocks = []
    for first in range(1, (ways + 1) // 2):
        angle = 2.0 * np.pi * (point * (first + ways * column) % length) / length
        cosine, sine = np.cos(angle), np.sin(angle)
        blocks.append(np.block([[cosine, -sine], [sine, cosine]]) / math.sqrt(LANES))
    block_high, block_low = split_bf16_numpy(np.stack(blocks))
    real = np.zeros((1, 2 * LANES, 2 * LANES), block_high.dtype)
    real[0, :LANES, :LANES], real[0, :LANES, LANES:] = split_bf16_numpy(real_block)
    return np.concatenate([block_high, block_low, real])


def dot_split(values, high_table, low_table, transposed):
    dims = (((1,), (1 if transposed else 0,)), ((), ()))
    count = values.shape[0]
    high, low = split_bf16(values)
    dot = functools.partial(lax.dot_general, dimension_numbers=dims, preferred_element_type=jnp.float32)
    main = dot(jnp.concatenate([high, low], axis=0), high_table)
    return main[:count] + (main[count:] + dot(high, low_table))


def damping_of(limit, wavenumber):
    ratio = limit / jnp.maximum(wavenumber, 1.0)
    return jnp.where(wavenumber > limit, ratio * ratio, 1.0)


def filter_kernel(sectors, edges, limit_ref, table, *refs):
    circle_refs = refs[:sectors]
    own_out, first_out, second_out = refs[sectors:sectors + 3]
    wide, real_wave, block_wave = refs[sectors + 3:]
    fields, levels, rows, width = circle_refs[0].shape
    sector = wide.shape[1] // sectors
    length = sector * sectors
    ways = length // LANES
    pairs = (ways - 1) // 2
    tiles = width // LANES
    per_field = levels * rows
    lat = lax.axis_index("lat")
    limit = limit_ref[...]

    for k in range(sectors):
        wide[:, k * sector:(k + 1) * sector] = circle_refs[k][:, :, :, :sector].reshape(fields * per_field, sector)

    @pl.when(jnp.min(limit) < length // 2)
    def _():
        lane = lax.broadcasted_iota(jnp.int32, (rows, LANES), 1)

        def forward(field, carry):
            span = pl.ds(pl.multiple_of(field * per_field, per_field), per_field)
            tile = [wide[span, a * LANES:(a + 1) * LANES] for a in range(ways)]
            even = [tile[a] + tile[ways - a] for a in range(1, pairs + 1)]
            odd = [tile[a] - tile[ways - a] for a in range(1, pairs + 1)]
            real_wave[span, :] = tile[0] + sum(even)
            for k in range(1, pairs + 1):
                turn = [2.0 * math.pi * (a * k % ways) / ways for a in range(1, pairs + 1)]
                block_wave[k - 1, span, :LANES] = tile[0] + sum(math.cos(t) * e for t, e in zip(turn, even))
                block_wave[k - 1, span, LANES:] = -sum(math.sin(t) * o for t, o in zip(turn, odd))
            return carry

        lax.fori_loop(0, fields, forward, 0)

        def damp(spectrum, damping):
            shaped = spectrum.reshape(fields * levels, rows, damping.shape[-1])
            return (shaped * damping[None]).reshape(spectrum.shape)

        half = LANES // 2
        wave = (jnp.where(lane <= half, lane, lane - half) * ways).astype(jnp.float32)
        real_high, real_low = table[2 * pairs, :LANES, :LANES], table[2 * pairs, :LANES, LANES:]
        spectrum = dot_split(real_wave[...], real_high, real_low, False)
        spectrum = damp(spectrum, damping_of(limit, wave))
        real_wave[...] = dot_split(spectrum, real_high, real_low, True)
        for k in range(1, pairs + 1):
            mode = k + ways * lane
            one = damping_of(limit, jnp.minimum(mode, length - mode).astype(jnp.float32))
            damping = jnp.concatenate([one, one], axis=1)
            high, low = table[k - 1], table[pairs + k - 1]
            spectrum = dot_split(block_wave[k - 1], high, low, False)
            block_wave[k - 1] = dot_split(damp(spectrum, damping), high, low, True)

        def backward(field, carry):
            span = pl.ds(pl.multiple_of(field * per_field, per_field), per_field)
            base = real_wave[span, :] * (1.0 / ways)
            cosines = [block_wave[k, span, :LANES] for k in range(pairs)]
            sines = [block_wave[k, span, LANES:] for k in range(pairs)]
            wide[span, :LANES] = base + (2.0 / ways) * sum(cosines)
            for a in range(1, pairs + 1):
                turn = [2.0 * math.pi * (a * k % ways) / ways for k in range(1, pairs + 1)]
                even = base + sum((2.0 / ways * math.cos(t)) * c for t, c in zip(turn, cosines))
                odd = sum((2.0 / ways * math.sin(t)) * s for t, s in zip(turn, sines))
                wide[span, a * LANES:(a + 1) * LANES] = even - odd
                wide[span, (ways - a) * LANES:(ways - a + 1) * LANES] = even + odd
            return carry

        lax.fori_loop(0, fields, backward, 0)

    def emit(field, carry):
        span = pl.ds(pl.multiple_of(field * per_field, per_field), per_field)
        lane = lax.broadcasted_iota(jnp.int32, (per_field, LANES), 1)
        for a in range(tiles):
            tile = wide[span, a * LANES:(a + 1) * LANES]
            if a == tiles - 1:
                behind = wide[span, (ways - 1) * LANES:]
                tile = jnp.where(lane >= LANES - HALO, behind, tile)
            turned = jnp.swapaxes(tile.reshape(levels, rows, LANES), 0, 1)
            own_out[pl.ds(field, 1), :, :, a * LANES:(a + 1) * LANES] = turned[None]
        return carry

    lax.fori_loop(0, fields, emit, 0)
    if edges:
        final = slice(width - LANES, width)
        ahead = jnp.swapaxes(circle_refs[1][0, :, :, final], 0, 1)
        behind = jnp.swapaxes(circle_refs[sectors - 1][0, :, :, final], 0, 1)
        first_lane = edge_lane(sector)
        lane = lax.broadcasted_iota(jnp.int32, (rows, levels, LANES), 2) - first_lane
        spare = jnp.where(lane % (2 * HALO) < HALO, ahead, behind)
        spare = jnp.where((lane >= 0) & (lane < RATES * 2 * HALO), spare, own_out[0, :, :, final])
        own_out[0, :, :, final] = spare

    top = rows - HALO
    to_next = lax.rem(lat, 2) == 0

    @pl.when(to_next)
    def _():
        first_out[...] = own_out[:, top:]
        second_out[...] = own_out[:, :HALO]

    @pl.when(jnp.logical_not(to_next))
    def _():
        first_out[...] = own_out[:, :HALO]
        second_out[...] = own_out[:, top:]


def edge_lane(sector):
    return sector % LANES + HALO


def limits_of(cutoff, rows):
    lat = lax.axis_index("lat")
    own = lax.dynamic_slice_in_dim(cutoff, lat * rows, rows, 0).astype(jnp.float32)
    return jnp.broadcast_to(own[:, None], (rows, LANES))


def pack_kernel(chunks, adjoint, *refs):
    sources = (adjoint,) + refs[:RATES]
    count = len(chunks)
    payloads = refs[RATES:RATES + count]
    own_out, first_out, second_out = refs[RATES + count:RATES + count + 3]
    state, rates, sems = refs[RATES + count + 3:]
    levels, rows, sector = sources[1].shape
    width = own_out.shape[-1]
    final = slice(width - LANES, width)
    tail = sector - (width - LANES)
    copies = [pltpu.make_async_copy(src, rates.at[q], sems.at[q]) for q, src in enumerate(sources[1:])]
    copies.append(pltpu.make_async_copy(adjoint, state, sems.at[RATES]))
    for copy in copies:
        copy.start()
    for copy in copies[:RATES]:
        copy.wait()
    lat = lax.axis_index("lat")
    is_last = lat == lax.axis_size("lat") - 1
    lane = lax.broadcasted_iota(jnp.int32, (levels, rows, LANES), 2)
    row = lax.broadcasted_iota(jnp.int32, (levels, rows, LANES), 1)
    edges = jnp.zeros((levels, rows, LANES), jnp.float32)
    for q in range(RATES):
        at = edge_lane(sector) + 2 * HALO * q
        for start in range(0, width, LANES):
            size = min(LANES, sector - start)
            tile = rates[q, :, :, start:start + size]
            if size < LANES:
                tile = jnp.concatenate([tile, jnp.zeros((levels, rows, LANES - size), jnp.float32)], axis=2)
            if q == 0:
                tile = jnp.where(jnp.logical_and(is_last, row == rows - 1), 0.0, tile)
            own_out[:, q, :, start:start + LANES] = jnp.swapaxes(tile, 0, 1)
            if start == 0:
                initial = pltpu.roll(tile, at, 2)
                edges = jnp.where((lane >= at) & (lane < at + HALO), initial, edges)
            if start == width - LANES:
                last = pltpu.roll(tile, (at + HALO - (tail - HALO)) % LANES, 2)
                edges = jnp.where((lane >= at + HALO) & (lane < at + 2 * HALO), last, edges)
    copies[RATES].wait()
    field = 0
    for c in range(count):
        for j in range(chunks[c]):
            payloads[c][j, :, :, :width - LANES] = state[field, :, :, :width - LANES]
            end = state[field, :, :, width - LANES:]
            end = jnp.concatenate([end, jnp.zeros((levels, rows, LANES - tail), jnp.float32)], axis=2)
            if field == 0:
                end = jnp.where(lane < tail, end, edges)
            payloads[c][j, :, :, final] = end
            field += 1
    top = rows - HALO
    to_next = lax.rem(lat, 2) == 0

    @pl.when(to_next)
    def _():
        first_out[...] = own_out[top:]
        second_out[...] = own_out[:HALO]

    @pl.when(jnp.logical_not(to_next))
    def _():
        first_out[...] = own_out[:HALO]
        second_out[...] = own_out[top:]


def by_side(first_ref, second_ref, use):
    to_next = lax.rem(lax.axis_index("lat"), 2) == 0

    @pl.when(to_next)
    def _():
        use(second_ref, first_ref)

    @pl.when(jnp.logical_not(to_next))
    def _():
        use(first_ref, second_ref)


def coupling_power(coupling_ref):
    fields, levels, _ = coupling_ref.shape
    base = []
    for g in range(fields):
        line = coupling_ref[g]
        base.append([jnp.broadcast_to(line[:, f:f + 1], (levels, LANES)) for f in range(fields)])
        base[g][g] = base[g][g] + 1.0

    def product(left, right):
        def entry(g, f):
            return functools.reduce(jnp.add, [left[g][h] * right[h][f] for h in range(fields)])

        return [[entry(g, f) for f in range(fields)] for g in range(fields)]

    power = base
    for bit in bin(SUBSTEPS)[3:]:
        power = product(power, power)
        if bit == "1":
            power = product(power, base)
    return power


def face_kernel(sector, coupling, rate_own, rate_first, rate_second, own, first, second, level, power_out):
    power = coupling_power(coupling)
    for g, entries in enumerate(power):
        for f, value in enumerate(entries):
            power_out[g, f] = value
    rows, kinds, levels, width = rate_own.shape
    extent = rows + 2 * HALO
    tiles = width // LANES
    final = slice(width - LANES, width)
    lane = lax.broadcasted_iota(jnp.int32, (levels, LANES), 1)
    end = sector % LANES

    def extend(ref, edge_ref, base):
        count = ref.shape[0]
        for q in range(kinds):
            at = edge_lane(sector) + 2 * HALO * q
            edges = [edge_ref[0, r, :, final] for r in range(count)]
            ahead = [pltpu.roll(e, (end - at) % LANES, 1) for e in edges]
            behind = [pltpu.roll(e, (LANES - HALO - at - HALO) % LANES, 1) for e in edges]
            for r in range(count):
                piece = jnp.where((lane >= end) & (lane < end + HALO), ahead[r], ref[r, q, :, final])
                piece = jnp.where(lane >= LANES - HALO, behind[r], piece)
                level[base + r, q, :, :width - LANES] = ref[r, q, :, :width - LANES]
                level[base + r, q, :, final] = piece

    extend(rate_own, own, HALO)

    def halos(below, above, below_edges, above_edges):
        extend(below, below_edges, 0)
        extend(above, above_edges, HALO + rows)

    to_next = lax.rem(lax.axis_index("lat"), 2) == 0

    @pl.when(to_next)
    def _():
        halos(rate_second, rate_first, second, first)

    @pl.when(jnp.logical_not(to_next))
    def _():
        halos(rate_first, rate_second, first, second)

    for r in range(extent - 2, 0, -1):
        west = shifted([level[r, 3, :, t * LANES:(t + 1) * LANES] for t in range(tiles)], 1)
        for t in range(tiles):
            span = slice(t * LANES, (t + 1) * LANES)
            north, south, east = level[r, 0, :, span], level[r - 1, 1, :, span], level[r, 2, :, span]
            level[r, 1, :, span] = south
            level[r, 3, :, span] = west[t]
            level[r, 4, :, span] = 1.0 - east - west[t] - north - south


def shifted(tiles, step):
    lane = lax.broadcasted_iota(jnp.int32, tiles[0].shape, 1)
    rolled = [pltpu.roll(tile, step % LANES, 1) for tile in tiles]
    border = lane == (0 if step == 1 else LANES - 1)
    count = len(tiles)
    return [jnp.where(border, rolled[(t - step) % count], rolled[t]) for t in range(count)]


def transport_kernel(chunk, finished, sector, power_ref, rates, own_ref, first_ref, second_ref, *refs):
    earlier = refs[:finished]
    out_ref, even, odd = refs[finished:]
    rows, levels, width = own_ref.shape[1:]
    extent = rows + 2 * HALO
    tiles = width // LANES
    last = finished > 0

    def put(ref, base):
        even[:, base:base + ref.shape[1]] = ref[...]

    put(own_ref, HALO)

    def halos(below, above):
        put(below, 0)
        put(above, HALO + rows)

    by_side(first_ref, second_ref, halos)

    def line(source, r, field):
        return [source[field, r, :, t * LANES:(t + 1) * LANES] for t in range(tiles)]

    for step in range(SUBSTEPS):
        source, target = (even, odd) if step % 2 == 0 else (odd, even)
        count = extent - 2 - 2 * step

        def finish(field, r, here, ahead, behind):
            for t in range(tiles):
                span = slice(t * LANES, (t + 1) * LANES)
                north, south, east, west, stay = (rates[r, q, :, span] for q in range(5))
                target[field, r, :, span] = (
                    (stay * here[t] + (north * source[field, r + 1, :, span] + south * source[field, r - 1, :, span]))
                    + (east * ahead[t] + west * behind[t])
                )

        def work(first, number, field):
            for r in [first + j for j in range(number)]:
                here = line(source, r, field)
                finish(field, r, here, shifted(here, -1), shifted(here, 1))

        for field in range(chunk):
            def group(index, carry):
                work(step + 1 + ROWS_AT_ONCE * index, ROWS_AT_ONCE, field)
                return carry

            groups, rest = count // ROWS_AT_ONCE, count % ROWS_AT_ONCE
            if groups > 1:
                lax.fori_loop(0, groups, group, 0)
            else:
                work(step + 1, groups * ROWS_AT_ONCE, field)
            work(step + 1 + groups * ROWS_AT_ONCE, rest, field)
    result = even if SUBSTEPS % 2 == 0 else odd

    if not last:
        out_ref[...] = result[:, HALO:HALO + rows]
        return
    sources = [(ref, j, 0) for ref in earlier for j in range(ref.shape[0])]
    sources += [(result, j, HALO) for j in range(chunk)]
    fields = len(sources)
    for start in range(0, sector, LANES):
        stop = min(start + LANES, sector)
        values = [ref[j, base:base + rows, :, start:start + LANES] for ref, j, base in sources]
        for f in range(fields):
            total = functools.reduce(jnp.add, [power_ref[g, f][None] * values[g] for g in range(fields)])
            out_ref[f, :, :, start:stop] = jnp.swapaxes(total, 0, 1)[:, :, :stop - start]


def lat_pairs(count):
    def both(start):
        ups = [(i, i + 1) for i in range(start, count - 1, 2)]
        return ups + [(j, i) for i, j in ups]

    return both(0), both(1)


def shards(adjoint_in, lat_ahead, lat_behind, lon_ahead, lon_behind, coupling, cutoff):
    fields, levels, rows, sector = adjoint_in.shape
    sectors = lax.axis_size("lon")
    length = sector * sectors
    width = -(-(sector + 2 * HALO) // LANES) * LANES
    even_pairs, odd_pairs = lat_pairs(lax.axis_size("lat"))
    f32 = jnp.float32
    chunks = CHUNKS if sum(CHUNKS) == fields else (fields,)

    def sector_ahead(values, offset):
        return lax.ppermute(values, "lon", [(s, (s - offset) % sectors) for s in range(sectors)])

    def to_bands(first, second):
        return lax.ppermute(first, "lat", even_pairs), lax.ppermute(second, "lat", odd_pairs)

    extent = rows + 2 * HALO
    rate_shape = (RATES, levels, width)
    *payloads, rate_own, rate_first, rate_second = pl.pallas_call(
        functools.partial(pack_kernel, chunks),
        out_shape=(
            *(jax.ShapeDtypeStruct((n, levels, rows, width), f32) for n in chunks),
            jax.ShapeDtypeStruct((rows,) + rate_shape, f32),
            jax.ShapeDtypeStruct((HALO,) + rate_shape, f32),
            jax.ShapeDtypeStruct((HALO,) + rate_shape, f32),
        ),
        in_specs=[HBM] * (1 + RATES),
        out_specs=(VMEM,) * (len(chunks) + 3),
        scratch_shapes=[
            pltpu.VMEM(adjoint_in.shape, f32),
            pltpu.VMEM((RATES,) + lat_ahead.shape, f32),
            pltpu.SemaphoreType.DMA((1 + RATES,)),
        ],
        compiler_params=PARAMS,
        name="pack",
    )(*(
        pltpu.with_memory_space_constraint(array, pltpu.HBM)
        for array in (adjoint_in, lat_ahead, lat_behind, lon_ahead, lon_behind)
    ))
    circles = [[part] + [sector_ahead(part, k) for k in range(1, sectors)] for part in payloads]
    rate_first, rate_second = to_bands(rate_first, rate_second)

    limits = limits_of(cutoff, rows)
    table = jnp.asarray(mode_tables(length))
    results = []
    for c, (n, circle) in enumerate(zip(chunks, circles)):
        lines = n * levels * rows
        own, first, second = pl.pallas_call(
            functools.partial(filter_kernel, sectors, c == 0),
            out_shape=(
                jax.ShapeDtypeStruct((n, rows, levels, width), f32),
                jax.ShapeDtypeStruct((n, HALO, levels, width), f32),
                jax.ShapeDtypeStruct((n, HALO, levels, width), f32),
            ),
            in_specs=[VMEM] * (sectors + 2),
            out_specs=(VMEM,) * 3,
            scratch_shapes=[
                pltpu.VMEM((lines, length), f32),
                pltpu.VMEM((lines, LANES), f32),
                pltpu.VMEM((table.shape[0] // 2, lines, 2 * LANES), f32),
            ],
            compiler_params=PARAMS,
            name="polar_filter",
        )(limits, table, *circle)
        first, second = to_bands(first, second)
        if c == 0:
            level, power = pl.pallas_call(
                functools.partial(face_kernel, sector),
                out_shape=(
                    jax.ShapeDtypeStruct((extent, 5, levels, width), f32),
                    jax.ShapeDtypeStruct((fields, fields, levels, LANES), f32),
                ),
                in_specs=[VMEM] * 7,
                out_specs=(VMEM,) * 2,
                compiler_params=PARAMS,
                name="faces",
            )(jnp.transpose(coupling, (1, 0, 2)), rate_own, rate_first, rate_second, own, first, second)
        is_last = c == len(chunks) - 1
        earlier = results if is_last else []
        shape = adjoint_in.shape if is_last else (n, rows, levels, width)
        results.append(pl.pallas_call(
            functools.partial(transport_kernel, n, len(earlier), sector),
            out_shape=jax.ShapeDtypeStruct(shape, f32),
            in_specs=[VMEM] * (5 + len(earlier)),
            out_specs=VMEM,
            scratch_shapes=[
                pltpu.VMEM((n, extent, levels, width), f32),
                pltpu.VMEM((n, extent, levels, width), f32),
            ],
            compiler_params=PARAMS,
            name="transport",
        )(power, level, own, first, second, *earlier))
    return results[-1]


def solution(mesh):
    placed = (
        P("member", "lev", "lat", "lon"),
        P(("member", "lev"), "lat", "lon"),
        P(("member", "lev"), "lat", "lon"),
        P(("member", "lev"), "lat", "lon"),
        P(("member", "lev"), "lat", "lon"),
        P("lev", None, None),
        P(),
    )
    return jax.shard_map(
        shards,
        mesh=mesh,
        in_specs=placed,
        out_specs=P("member", "lev", "lat", "lon"),
        check_vma=False,
    )
```

```python
import functools
import math

import jax
import jax.numpy as jnp
import numpy as np
from jax import lax
from jax.experimental import pallas as pl
from jax.experimental.pallas import tpu as pltpu
from jax.sharding import PartitionSpec as P

SUBSTEPS = 6
HALO = SUBSTEPS
LANES = 128
RATES = 4
CHUNKS = (3, 2)
ROWS_AT_ONCE = 9
PARAMS = pltpu.CompilerParams(vmem_limit_bytes=12 * 2**20)
VMEM = pl.BlockSpec(memory_space=pltpu.VMEM)
HBM = pl.BlockSpec(memory_space=pltpu.HBM)


def split_bf16(values):
    high = values.astype(jnp.bfloat16)
    low = (values - high.astype(jnp.float32)).astype(jnp.bfloat16)
    return high, low


def split_bf16_numpy(values):
    values = values.astype(np.float32)
    high = values.astype(jnp.bfloat16)
    low = (values - high.astype(np.float32)).astype(jnp.bfloat16)
    return high, low


def mode_tables(length):
    ways = length // LANES
    point = np.arange(LANES)[:, None].astype(np.int64)
    column = np.arange(LANES)[None, :].astype(np.int64)
    half = LANES // 2
    wave = np.where(column <= half, column, column - half)
    angle = 2.0 * np.pi * (point * wave % LANES) / LANES
    weight = np.where((column == 0) | (column == half), 1.0 / LANES, 2.0 / LANES)
    real_block = np.where(column <= half, np.cos(angle), np.sin(angle)) * np.sqrt(weight)
    blocks = []
    for first in range(1, (ways + 1) // 2):
        angle = 2.0 * np.pi * (point * (first + ways * column) % length) / length
        cosine, sine = np.cos(angle), np.sin(angle)
        blocks.append(np.block([[cosine, -sine], [sine, cosine]]) / math.sqrt(LANES))
    block_high, block_low = split_bf16_numpy(np.stack(blocks))
    real = np.zeros((1, 2 * LANES, 2 * LANES), block_high.dtype)
    real[0, :LANES, :LANES], real[0, :LANES, LANES:] = split_bf16_numpy(real_block)
    return np.concatenate([block_high, block_low, real])


def dot_split(values, high_table, low_table, transposed):
    dims = (((1,), (1 if transposed else 0,)), ((), ()))
    count = values.shape[0]
    high, low = split_bf16(values)
    dot = functools.partial(lax.dot_general, dimension_numbers=dims, preferred_element_type=jnp.float32)
    main = dot(jnp.concatenate([high, low], axis=0), high_table)
    return main[:count] + (main[count:] + dot(high, low_table))


def damping_of(limit, wavenumber):
    ratio = limit / jnp.maximum(wavenumber, 1.0)
    return jnp.where(wavenumber > limit, ratio * ratio, 1.0)


def filter_kernel(sectors, edges, limit_ref, table, *refs):
    circle_refs = refs[:sectors]
    own_out, first_out, second_out = refs[sectors:sectors + 3]
    wide, real_wave, block_wave = refs[sectors + 3:]
    fields, levels, rows, width = circle_refs[0].shape
    ways = wide.shape[0]
    length = ways * LANES
    sector = length // sectors
    pairs = (ways - 1) // 2
    tiles = width // LANES
    per_field = levels * rows
    lat = lax.axis_index("lat")
    limit = limit_ref[...]

    lines = fields * per_field
    line_lane = lax.broadcasted_iota(jnp.int32, (lines, LANES), 1)
    rolled = {}

    def part(k, t):
        if (k, t) not in rolled:
            tile = circle_refs[k][:, :, :, t * LANES:(t + 1) * LANES].reshape(lines, LANES)
            offset = k * sector % LANES
            rolled[k, t] = pltpu.roll(tile, offset, 1) if offset else tile
        return rolled[k, t]

    def assemble(a):
        tile = None
        for k in range(sectors):
            low, high = k * sector, (k + 1) * sector
            if high <= a * LANES or low >= (a + 1) * LANES:
                continue
            t, offset = a - low // LANES, low % LANES
            here = part(k, t) if t * LANES < sector else part(k, t - 1)
            if offset and t > 0 and t * LANES < sector:
                here = jnp.where(line_lane < offset, part(k, t - 1), here)
            tile = here if tile is None else jnp.where(line_lane < low - a * LANES, tile, here)
        wide[a] = tile

    for a in range(ways):
        if a < tiles or a == ways - 1:
            assemble(a)

    @pl.when(jnp.min(limit) < length // 2)
    def _():
        rolled.clear()
        for a in range(tiles, ways - 1):
            assemble(a)
        lane = lax.broadcasted_iota(jnp.int32, (rows, LANES), 1)

        def forward(field, carry):
            span = pl.ds(pl.multiple_of(field * per_field, per_field), per_field)
            tile = [wide[a, span, :] for a in range(ways)]
            even = [tile[a] + tile[ways - a] for a in range(1, pairs + 1)]
            odd = [tile[a] - tile[ways - a] for a in range(1, pairs + 1)]
            real_wave[span, :] = tile[0] + sum(even)
            for k in range(1, pairs + 1):
                turn = [2.0 * math.pi * (a * k % ways) / ways for a in range(1, pairs + 1)]
                block_wave[k - 1, span, :LANES] = tile[0] + sum(math.cos(t) * e for t, e in zip(turn, even))
                block_wave[k - 1, span, LANES:] = -sum(math.sin(t) * o for t, o in zip(turn, odd))
            return carry

        lax.fori_loop(0, fields, forward, 0)

        def damp(spectrum, damping):
            shaped = spectrum.reshape(fields * levels, rows, damping.shape[-1])
            return (shaped * damping[None]).reshape(spectrum.shape)

        half = LANES // 2
        wave = (jnp.where(lane <= half, lane, lane - half) * ways).astype(jnp.float32)
        real_high, real_low = table[2 * pairs, :LANES, :LANES], table[2 * pairs, :LANES, LANES:]
        spectrum = dot_split(real_wave[...], real_high, real_low, False)
        spectrum = damp(spectrum, damping_of(limit, wave))
        real_wave[...] = dot_split(spectrum, real_high, real_low, True)
        for k in range(1, pairs + 1):
            mode = k + ways * lane
            one = damping_of(limit, jnp.minimum(mode, length - mode).astype(jnp.float32))
            damping = jnp.concatenate([one, one], axis=1)
            high, low = table[k - 1], table[pairs + k - 1]
            spectrum = dot_split(block_wave[k - 1], high, low, False)
            block_wave[k - 1] = dot_split(damp(spectrum, damping), high, low, True)

        def backward(field, carry):
            span = pl.ds(pl.multiple_of(field * per_field, per_field), per_field)
            base = real_wave[span, :] * (1.0 / ways)
            cosines = [block_wave[k, span, :LANES] for k in range(pairs)]
            sines = [block_wave[k, span, LANES:] for k in range(pairs)]
            wide[0, span, :] = base + (2.0 / ways) * sum(cosines)
            for a in range(1, pairs + 1):
                turn = [2.0 * math.pi * (a * k % ways) / ways for k in range(1, pairs + 1)]
                even = base + sum((2.0 / ways * math.cos(t)) * c for t, c in zip(turn, cosines))
                odd = sum((2.0 / ways * math.sin(t)) * s for t, s in zip(turn, sines))
                wide[a, span, :] = even - odd
                if a == 1 or ways - a < tiles:
                    wide[ways - a, span, :] = even + odd
            return carry

        lax.fori_loop(0, fields, backward, 0)

    def emit(field, carry):
        lane = lax.broadcasted_iota(jnp.int32, (levels, LANES), 1)
        for r in range(rows):
            span = pl.ds(field * per_field + r, levels, stride=rows)
            for a in range(tiles):
                tile = wide[a, span, :]
                if a == tiles - 1:
                    behind = wide[ways - 1, span, :]
                    tile = jnp.where(lane >= LANES - HALO, behind, tile)
                own_out[field, r, :, a * LANES:(a + 1) * LANES] = tile
        return carry

    lax.fori_loop(0, fields, emit, 0)
    if edges:
        final = slice(width - LANES, width)
        ahead = jnp.swapaxes(circle_refs[1][0, :, :, final], 0, 1)
        behind = jnp.swapaxes(circle_refs[sectors - 1][0, :, :, final], 0, 1)
        first_lane = edge_lane(sector)
        lane = lax.broadcasted_iota(jnp.int32, (rows, levels, LANES), 2) - first_lane
        spare = jnp.where(lane % (2 * HALO) < HALO, ahead, behind)
        spare = jnp.where((lane >= 0) & (lane < RATES * 2 * HALO), spare, own_out[0, :, :, final])
        own_out[0, :, :, final] = spare

    top = rows - HALO
    to_next = lax.rem(lat, 2) == 0

    @pl.when(to_next)
    def _():
        first_out[...] = own_out[:, top:]
        second_out[...] = own_out[:, :HALO]

    @pl.when(jnp.logical_not(to_next))
    def _():
        first_out[...] = own_out[:, :HALO]
        second_out[...] = own_out[:, top:]


def edge_lane(sector):
    return sector % LANES + HALO


def limits_of(cutoff, rows):
    lat = lax.axis_index("lat")
    own = lax.dynamic_slice_in_dim(cutoff, lat * rows, rows, 0).astype(jnp.float32)
    return jnp.broadcast_to(own[:, None], (rows, LANES))


def write_state(state, payload, field, extra):
    levels, rows, sector = state.shape[1:]
    width = payload.shape[-1]
    tail = sector - (width - LANES)
    payload[field, :, :, :width - LANES] = state[field, :, :, :width - LANES]
    end = jnp.concatenate([state[field, :, :, width - LANES:], extra[:, :, tail:]], axis=2)
    payload[field, :, :, width - LANES:] = end


def first_pack_kernel(adjoint, *refs):
    sources, (payload, state, rates, sems) = refs[:RATES], refs[RATES:]
    count, levels, rows, width = payload.shape
    sector = state.shape[-1]
    tail = sector - (width - LANES)
    copies = [pltpu.make_async_copy(adjoint.at[:count], state, sems.at[RATES])]
    for q, source in enumerate(sources):
        copies.append(pltpu.make_async_copy(source, rates.at[q], sems.at[q]))
    for copy in copies:
        copy.start()
    for copy in copies[1:]:
        copy.wait()
    lat = lax.axis_index("lat")
    top = jnp.where(lat == lax.axis_size("lat") - 1, rows - 1, rows)
    lane = lax.broadcasted_iota(jnp.int32, (levels, rows, LANES), 2)
    row = lax.broadcasted_iota(jnp.int32, (levels, rows, LANES), 1)
    edges = jnp.zeros((levels, rows, LANES), jnp.float32)
    for q in range(RATES):
        at = edge_lane(sector) + 2 * HALO * q
        head = pltpu.roll(rates[q, :, :, :LANES], at, 2)
        end = jnp.concatenate([rates[q, :, :, width - LANES:], jnp.zeros((levels, rows, LANES - tail), jnp.float32)], axis=2)
        end = pltpu.roll(end, (at + HALO - (tail - HALO)) % LANES, 2)
        if q == 0:
            head, end = jnp.where(row < top, head, 0.0), jnp.where(row < top, end, 0.0)
        edges = jnp.where((lane >= at) & (lane < at + HALO), head, edges)
        edges = jnp.where((lane >= at + HALO) & (lane < at + 2 * HALO), end, edges)
    copies[0].wait()
    zero = jnp.zeros((levels, rows, LANES), jnp.float32)
    for field in range(count):
        write_state(state, payload, field, edges if field == 0 else zero)


def rest_pack_kernel(chunks, adjoint, *refs):
    sources = refs[:RATES]
    count = len(chunks) - 1
    payloads = refs[RATES:RATES + count]
    own_out, first_out, second_out = refs[RATES + count:RATES + count + 3]
    state, rates, sems = refs[RATES + count + 3:]
    levels, rows, sector = sources[0].shape
    width = own_out.shape[-1]
    copies = [pltpu.make_async_copy(src, rates.at[q], sems.at[q]) for q, src in enumerate(sources)]
    if count:
        copies.append(pltpu.make_async_copy(adjoint.at[chunks[0]:], state, sems.at[RATES]))
    for copy in copies:
        copy.start()
    for copy in copies[:RATES]:
        copy.wait()
    lat = lax.axis_index("lat")
    is_last = lat == lax.axis_size("lat") - 1
    row = lax.broadcasted_iota(jnp.int32, (levels, rows, LANES), 1)
    for q in range(RATES):
        for start in range(0, width, LANES):
            size = min(LANES, sector - start)
            tile = rates[q, :, :, start:start + size]
            if size < LANES:
                tile = jnp.concatenate([tile, jnp.zeros((levels, rows, LANES - size), jnp.float32)], axis=2)
            if q == 0:
                tile = jnp.where(jnp.logical_and(is_last, row == rows - 1), 0.0, tile)
            own_out[:, q, :, start:start + LANES] = jnp.swapaxes(tile, 0, 1)
    if count:
        copies[RATES].wait()
    zero = jnp.zeros((levels, rows, LANES), jnp.float32)
    at = 0
    for c in range(count):
        for j in range(chunks[c + 1]):
            write_state(state.at[at:at + 1], payloads[c].at[j:j + 1], 0, zero)
            at += 1
    top = rows - HALO
    to_next = lax.rem(lat, 2) == 0

    @pl.when(to_next)
    def _():
        first_out[...] = own_out[top:]
        second_out[...] = own_out[:HALO]

    @pl.when(jnp.logical_not(to_next))
    def _():
        first_out[...] = own_out[:HALO]
        second_out[...] = own_out[top:]


def by_side(first_ref, second_ref, use):
    to_next = lax.rem(lax.axis_index("lat"), 2) == 0

    @pl.when(to_next)
    def _():
        use(second_ref, first_ref)

    @pl.when(jnp.logical_not(to_next))
    def _():
        use(first_ref, second_ref)


def coupling_power(coupling_ref):
    fields, levels, _ = coupling_ref.shape
    base = []
    for g in range(fields):
        line = coupling_ref[g]
        base.append([jnp.broadcast_to(line[:, f:f + 1], (levels, LANES)) for f in range(fields)])
        base[g][g] = base[g][g] + 1.0

    def product(left, right):
        def entry(g, f):
            return functools.reduce(jnp.add, [left[g][h] * right[h][f] for h in range(fields)])

        return [[entry(g, f) for f in range(fields)] for g in range(fields)]

    power = base
    for bit in bin(SUBSTEPS)[3:]:
        power = product(power, power)
        if bit == "1":
            power = product(power, base)
    return power


def face_kernel(sector, coupling, rate_own, rate_first, rate_second, own, first, second, level, power_out):
    power = coupling_power(coupling)
    for g, entries in enumerate(power):
        for f, value in enumerate(entries):
            power_out[g, f] = value
    rows, kinds, levels, width = rate_own.shape
    extent = rows + 2 * HALO
    tiles = width // LANES
    final = slice(width - LANES, width)
    lane = lax.broadcasted_iota(jnp.int32, (levels, LANES), 1)
    end = sector % LANES

    def extend(ref, edge_ref, base):
        count = ref.shape[0]
        for q in range(kinds):
            at = edge_lane(sector) + 2 * HALO * q
            edges = [edge_ref[0, r, :, final] for r in range(count)]
            ahead = [pltpu.roll(e, (end - at) % LANES, 1) for e in edges]
            behind = [pltpu.roll(e, (LANES - HALO - at - HALO) % LANES, 1) for e in edges]
            for r in range(count):
                piece = jnp.where((lane >= end) & (lane < end + HALO), ahead[r], ref[r, q, :, final])
                piece = jnp.where(lane >= LANES - HALO, behind[r], piece)
                level[base + r, q, :, :width - LANES] = ref[r, q, :, :width - LANES]
                level[base + r, q, :, final] = piece

    extend(rate_own, own, HALO)

    def halos(below, above, below_edges, above_edges):
        extend(below, below_edges, 0)
        extend(above, above_edges, HALO + rows)

    to_next = lax.rem(lax.axis_index("lat"), 2) == 0

    @pl.when(to_next)
    def _():
        halos(rate_second, rate_first, second, first)

    @pl.when(jnp.logical_not(to_next))
    def _():
        halos(rate_first, rate_second, first, second)

    for r in range(extent - 2, 0, -1):
        west = shifted([level[r, 3, :, t * LANES:(t + 1) * LANES] for t in range(tiles)], 1)
        for t in range(tiles):
            span = slice(t * LANES, (t + 1) * LANES)
            north, south, east = level[r, 0, :, span], level[r - 1, 1, :, span], level[r, 2, :, span]
            level[r, 1, :, span] = south
            level[r, 3, :, span] = west[t]
            level[r, 4, :, span] = 1.0 - east - west[t] - north - south


def shifted(tiles, step):
    lane = lax.broadcasted_iota(jnp.int32, tiles[0].shape, 1)
    rolled = [pltpu.roll(tile, step % LANES, 1) for tile in tiles]
    border = lane == (0 if step == 1 else LANES - 1)
    count = len(tiles)
    return [jnp.where(border, rolled[(t - step) % count], rolled[t]) for t in range(count)]


def transport_kernel(chunk, finished, sector, power_ref, rates, own_ref, first_ref, second_ref, *refs):
    earlier = refs[:finished]
    out_ref, even, odd, stage = refs[finished:]
    rows, levels, width = own_ref.shape[1:]
    extent = rows + 2 * HALO
    tiles = width // LANES
    last = finished > 0

    def put(ref, base):
        even[:, base:base + ref.shape[1]] = ref[...]

    put(own_ref, HALO)

    def halos(below, above):
        put(below, 0)
        put(above, HALO + rows)

    by_side(first_ref, second_ref, halos)

    def line(source, r, field):
        return [source[field, r, :, t * LANES:(t + 1) * LANES] for t in range(tiles)]

    for step in range(SUBSTEPS):
        source, target = (even, odd) if step % 2 == 0 else (odd, even)
        count = extent - 2 - 2 * step

        def finish(field, r, here, ahead, behind):
            for t in range(tiles):
                span = slice(t * LANES, (t + 1) * LANES)
                north, south, east, west, stay = (rates[r, q, :, span] for q in range(5))
                target[field, r, :, span] = (
                    (stay * here[t] + (north * source[field, r + 1, :, span] + south * source[field, r - 1, :, span]))
                    + (east * ahead[t] + west * behind[t])
                )

        def work(first, number, field):
            for r in [first + j for j in range(number)]:
                here = line(source, r, field)
                finish(field, r, here, shifted(here, -1), shifted(here, 1))

        for field in range(chunk):
            def group(index, carry):
                work(step + 1 + ROWS_AT_ONCE * index, ROWS_AT_ONCE, field)
                return carry

            groups, rest = count // ROWS_AT_ONCE, count % ROWS_AT_ONCE
            if groups > 1:
                lax.fori_loop(0, groups, group, 0)
            else:
                work(step + 1, groups * ROWS_AT_ONCE, field)
            work(step + 1 + groups * ROWS_AT_ONCE, rest, field)
    result = even if SUBSTEPS % 2 == 0 else odd

    if not last:
        out_ref[...] = result[:, HALO:HALO + rows]
        return
    sources = [(ref, j, 0) for ref in earlier for j in range(ref.shape[0])]
    sources += [(result, j, HALO) for j in range(chunk)]
    fields = len(sources)
    def mix(f, carry):
        for start in range(0, sector, LANES):
            stop = min(start + LANES, sector)
            for r in range(rows):
                terms = [power_ref[g, f] * ref[j, base + r, :, start:start + LANES]
                         for g, (ref, j, base) in enumerate(sources)]
                stage[start // LANES, r * levels:(r + 1) * levels] = functools.reduce(jnp.add, terms)
            for level in range(levels):
                value = stage[start // LANES, pl.ds(level, rows, stride=levels), :]
                out_ref[f, level, :, start:stop] = value[:, :stop - start]
        return carry

    lax.fori_loop(0, fields, mix, 0)


def lat_pairs(count):
    def both(start):
        ups = [(i, i + 1) for i in range(start, count - 1, 2)]
        return ups + [(j, i) for i, j in ups]

    return both(0), both(1)


def shards(adjoint_in, lat_ahead, lat_behind, lon_ahead, lon_behind, coupling, cutoff):
    fields, levels, rows, sector = adjoint_in.shape
    sectors = lax.axis_size("lon")
    length = sector * sectors
    width = -(-(sector + 2 * HALO) // LANES) * LANES
    even_pairs, odd_pairs = lat_pairs(lax.axis_size("lat"))
    f32 = jnp.float32
    chunks = CHUNKS if sum(CHUNKS) == fields else (fields,)

    def sector_ahead(values, offset):
        return lax.ppermute(values, "lon", [(s, (s - offset) % sectors) for s in range(sectors)])

    def to_bands(first, second):
        return lax.ppermute(first, "lat", even_pairs), lax.ppermute(second, "lat", odd_pairs)

    extent = rows + 2 * HALO
    rate_shape = (RATES, levels, width)
    inputs = [
        pltpu.with_memory_space_constraint(array, pltpu.HBM)
        for array in (adjoint_in, lat_ahead, lat_behind, lon_ahead, lon_behind)
    ]
    payload_shapes = [jax.ShapeDtypeStruct((n, levels, rows, width), f32) for n in chunks]
    later = max(fields - chunks[0], 1)
    first_payload = pl.pallas_call(
        first_pack_kernel,
        out_shape=payload_shapes[0],
        in_specs=[HBM] * (1 + RATES),
        out_specs=VMEM,
        scratch_shapes=[
            pltpu.VMEM((chunks[0],) + adjoint_in.shape[1:], f32),
            pltpu.VMEM((RATES,) + lat_ahead.shape, f32),
            pltpu.SemaphoreType.DMA((1 + RATES,)),
        ],
        compiler_params=PARAMS,
        name="first_pack",
    )(*inputs)
    first_circle = [first_payload] + [sector_ahead(first_payload, k) for k in range(1, sectors)]
    *payloads, rate_own, rate_first, rate_second = pl.pallas_call(
        functools.partial(rest_pack_kernel, chunks),
        out_shape=(
            *payload_shapes[1:],
            jax.ShapeDtypeStruct((rows,) + rate_shape, f32),
            jax.ShapeDtypeStruct((HALO,) + rate_shape, f32),
            jax.ShapeDtypeStruct((HALO,) + rate_shape, f32),
        ),
        in_specs=[HBM] * (1 + RATES),
        out_specs=(VMEM,) * (len(chunks) + 2),
        scratch_shapes=[
            pltpu.VMEM((later,) + adjoint_in.shape[1:], f32),
            pltpu.VMEM((RATES,) + lat_ahead.shape, f32),
            pltpu.SemaphoreType.DMA((1 + RATES,)),
        ],
        compiler_params=PARAMS,
        name="rest_pack",
    )(*inputs)
    circles = [[part] + [sector_ahead(part, k) for k in range(1, sectors)] for part in payloads]
    circles.insert(0, first_circle)
    rate_first, rate_second = to_bands(rate_first, rate_second)

    limits = limits_of(cutoff, rows)
    table = jnp.asarray(mode_tables(length))
    results = []
    for c, (n, circle) in enumerate(zip(chunks, circles)):
        lines = n * levels * rows
        own, first, second = pl.pallas_call(
            functools.partial(filter_kernel, sectors, c == 0),
            out_shape=(
                jax.ShapeDtypeStruct((n, rows, levels, width), f32),
                jax.ShapeDtypeStruct((n, HALO, levels, width), f32),
                jax.ShapeDtypeStruct((n, HALO, levels, width), f32),
            ),
            in_specs=[VMEM] * (sectors + 2),
            out_specs=(VMEM,) * 3,
            scratch_shapes=[
                pltpu.VMEM((length // LANES, lines, LANES), f32),
                pltpu.VMEM((lines, LANES), f32),
                pltpu.VMEM((table.shape[0] // 2, lines, 2 * LANES), f32),
            ],
            compiler_params=PARAMS,
            name="polar_filter",
        )(limits, table, *circle)
        first, second = to_bands(first, second)
        if c == 0:
            level, power = pl.pallas_call(
                functools.partial(face_kernel, sector),
                out_shape=(
                    jax.ShapeDtypeStruct((extent, 5, levels, width), f32),
                    jax.ShapeDtypeStruct((fields, fields, levels, LANES), f32),
                ),
                in_specs=[VMEM] * 7,
                out_specs=(VMEM,) * 2,
                compiler_params=PARAMS,
                name="faces",
            )(jnp.transpose(coupling, (1, 0, 2)), rate_own, rate_first, rate_second, own, first, second)
        is_last = c == len(chunks) - 1
        earlier = results if is_last else []
        shape = adjoint_in.shape if is_last else (n, rows, levels, width)
        results.append(pl.pallas_call(
            functools.partial(transport_kernel, n, len(earlier), sector),
            out_shape=jax.ShapeDtypeStruct(shape, f32),
            in_specs=[VMEM] * (5 + len(earlier)),
            out_specs=VMEM,
            scratch_shapes=[
                pltpu.VMEM((n, extent, levels, width), f32),
                pltpu.VMEM((n, extent, levels, width), f32),
                pltpu.VMEM((width // LANES, rows * levels, LANES), f32),
            ],
            compiler_params=PARAMS,
            name="transport",
        )(power, level, own, first, second, *earlier))
    return results[-1]


def solution(mesh):
    placed = (
        P("member", "lev", "lat", "lon"),
        P(("member", "lev"), "lat", "lon"),
        P(("member", "lev"), "lat", "lon"),
        P(("member", "lev"), "lat", "lon"),
        P(("member", "lev"), "lat", "lon"),
        P("lev", None, None),
        P(),
    )
    return jax.shard_map(
        shards,
        mesh=mesh,
        in_specs=placed,
        out_specs=P("member", "lev", "lat", "lon"),
        check_vma=False,
    )
```

```python
import functools
import math

import jax
import jax.numpy as jnp
import numpy as np
from jax import lax
from jax.experimental import pallas as pl
from jax.experimental.pallas import tpu as pltpu
from jax.sharding import PartitionSpec as P

SUBSTEPS = 6
HALO = SUBSTEPS
LANES = 128
RATES = 4
CHUNKS = (3, 2)
ROWS_AT_ONCE = 9
PARAMS = pltpu.CompilerParams(vmem_limit_bytes=12 * 2**20)
VMEM = pl.BlockSpec(memory_space=pltpu.VMEM)
HBM = pl.BlockSpec(memory_space=pltpu.HBM)


def split_bf16(values):
    high = values.astype(jnp.bfloat16)
    low = (values - high.astype(jnp.float32)).astype(jnp.bfloat16)
    return high, low


def split_bf16_numpy(values):
    values = values.astype(np.float32)
    high = values.astype(jnp.bfloat16)
    low = (values - high.astype(np.float32)).astype(jnp.bfloat16)
    return high, low


def mode_tables(length):
    ways = length // LANES
    point = np.arange(LANES)[:, None].astype(np.int64)
    column = np.arange(LANES)[None, :].astype(np.int64)
    half = LANES // 2
    wave = np.where(column <= half, column, column - half)
    angle = 2.0 * np.pi * (point * wave % LANES) / LANES
    weight = np.where((column == 0) | (column == half), 1.0 / LANES, 2.0 / LANES)
    real_block = np.where(column <= half, np.cos(angle), np.sin(angle)) * np.sqrt(weight)
    blocks = []
    for first in range(1, (ways + 1) // 2):
        angle = 2.0 * np.pi * (point * (first + ways * column) % length) / length
        cosine, sine = np.cos(angle), np.sin(angle)
        blocks.append(np.block([[cosine, -sine], [sine, cosine]]) / math.sqrt(LANES))
    block_high, block_low = split_bf16_numpy(np.stack(blocks))
    real = np.zeros((1, 2 * LANES, 2 * LANES), block_high.dtype)
    real[0, :LANES, :LANES], real[0, :LANES, LANES:] = split_bf16_numpy(real_block)
    return np.concatenate([block_high, block_low, real])


def dot_split(values, high_table, low_table, transposed):
    dims = (((1,), (1 if transposed else 0,)), ((), ()))
    count = values.shape[0]
    high, low = split_bf16(values)
    dot = functools.partial(lax.dot_general, dimension_numbers=dims, preferred_element_type=jnp.float32)
    main = dot(jnp.concatenate([high, low], axis=0), high_table)
    return main[:count] + (main[count:] + dot(high, low_table))


def damping_of(limit, wavenumber):
    ratio = limit / jnp.maximum(wavenumber, 1.0)
    return jnp.where(wavenumber > limit, ratio * ratio, 1.0)


def filter_kernel(sectors, edges, limit_ref, table, *refs):
    circle_refs = refs[:sectors]
    own_out, first_out, second_out = refs[sectors:sectors + 3]
    wide, sums = refs[sectors + 3:]
    fields, levels, rows, width = circle_refs[0].shape
    ways = wide.shape[0]
    length = ways * LANES
    sector = length // sectors
    pairs = (ways - 1) // 2
    tiles = width // LANES
    per_field = levels * rows
    lat = lax.axis_index("lat")
    limit = limit_ref[...]

    lines = fields * per_field
    line_lane = lax.broadcasted_iota(jnp.int32, (lines, LANES), 1)
    rolled = {}

    def part(k, t):
        if (k, t) not in rolled:
            tile = circle_refs[k][:, :, :, t * LANES:(t + 1) * LANES].reshape(lines, LANES)
            offset = k * sector % LANES
            rolled[k, t] = pltpu.roll(tile, offset, 1) if offset else tile
        return rolled[k, t]

    def assemble(a):
        tile = None
        for k in range(sectors):
            low, high = k * sector, (k + 1) * sector
            if high <= a * LANES or low >= (a + 1) * LANES:
                continue
            t, offset = a - low // LANES, low % LANES
            here = part(k, t) if t * LANES < sector else part(k, t - 1)
            if offset and t > 0 and t * LANES < sector:
                here = jnp.where(line_lane < offset, part(k, t - 1), here)
            tile = here if tile is None else jnp.where(line_lane < low - a * LANES, tile, here)
        wide[a] = tile

    for a in range(ways):
        if a < tiles or a == ways - 1:
            assemble(a)

    @pl.when(jnp.min(limit) < length // 2)
    def _():
        rolled.clear()
        for a in range(tiles, ways - 1):
            assemble(a)
        lane = lax.broadcasted_iota(jnp.int32, (rows, LANES), 1)

        def damp(spectrum, damping):
            shaped = spectrum.reshape(fields * levels, rows, damping.shape[-1])
            return (shaped * damping[None]).reshape(spectrum.shape)

        folds = range(1, pairs + 1)
        wanted = [a for a in folds if a == 1 or a < tiles or ways - a < tiles]
        origin = wide[0]
        total = origin
        for a in folds:
            low, high = wide[a], wide[ways - a]
            wide[a], wide[ways - a] = low + high, low - high
            total = total + wide[a]
        half = LANES // 2
        wave = (jnp.where(lane <= half, lane, lane - half) * ways).astype(jnp.float32)
        real_high, real_low = table[2 * pairs, :LANES, :LANES], table[2 * pairs, :LANES, LANES:]
        spectrum = damp(dot_split(total, real_high, real_low, False), damping_of(limit, wave))
        base = dot_split(spectrum, real_high, real_low, True) * (1.0 / ways)
        for k in folds:
            turn = [2.0 * math.pi * (a * k % ways) / ways for a in folds]
            cosines = wide[0] + sum(math.cos(t) * wide[a] for t, a in zip(turn, folds))
            sines = -sum(math.sin(t) * wide[ways - a] for t, a in zip(turn, folds))
            mode = k + ways * lane
            one = damping_of(limit, jnp.minimum(mode, length - mode).astype(jnp.float32))
            damping = jnp.concatenate([one, one], axis=1) * (2.0 / ways)
            high, low = table[k - 1], table[pairs + k - 1]
            spectrum = dot_split(jnp.concatenate([cosines, sines], axis=1), high, low, False)
            wave_back = dot_split(damp(spectrum, damping), high, low, True)
            cosines, sines = wave_back[:, :LANES], wave_back[:, LANES:]
            sums[0] = (base if k == 1 else sums[0]) + cosines
            for a in wanted:
                t = 2.0 * math.pi * (a * k % ways) / ways
                sums[a] = (base if k == 1 else sums[a]) + math.cos(t) * cosines
                part_sines = math.sin(t) * sines
                sums[pairs + a] = part_sines if k == 1 else sums[pairs + a] + part_sines
        wide[0] = sums[0]
        for a in wanted:
            if a < tiles:
                wide[a] = sums[a] - sums[pairs + a]
            if a == 1 or ways - a < tiles:
                wide[ways - a] = sums[a] + sums[pairs + a]

    def emit(field, carry):
        lane = lax.broadcasted_iota(jnp.int32, (levels, LANES), 1)
        for r in range(rows):
            span = pl.ds(field * per_field + r, levels, stride=rows)
            for a in range(tiles):
                tile = wide[a, span, :]
                if a == tiles - 1:
                    behind = wide[ways - 1, span, :]
                    tile = jnp.where(lane >= LANES - HALO, behind, tile)
                own_out[field, r, :, a * LANES:(a + 1) * LANES] = tile
        return carry

    lax.fori_loop(0, fields, emit, 0)
    if edges:
        final = slice(width - LANES, width)
        ahead = jnp.swapaxes(circle_refs[1][0, :, :, final], 0, 1)
        behind = jnp.swapaxes(circle_refs[sectors - 1][0, :, :, final], 0, 1)
        first_lane = edge_lane(sector)
        lane = lax.broadcasted_iota(jnp.int32, (rows, levels, LANES), 2) - first_lane
        spare = jnp.where(lane % (2 * HALO) < HALO, ahead, behind)
        spare = jnp.where((lane >= 0) & (lane < RATES * 2 * HALO), spare, own_out[0, :, :, final])
        own_out[0, :, :, final] = spare

    top = rows - HALO
    to_next = lax.rem(lat, 2) == 0

    @pl.when(to_next)
    def _():
        first_out[...] = own_out[:, top:]
        second_out[...] = own_out[:, :HALO]

    @pl.when(jnp.logical_not(to_next))
    def _():
        first_out[...] = own_out[:, :HALO]
        second_out[...] = own_out[:, top:]


def edge_lane(sector):
    return sector % LANES + HALO


def limits_of(cutoff, rows):
    lat = lax.axis_index("lat")
    own = lax.dynamic_slice_in_dim(cutoff, lat * rows, rows, 0).astype(jnp.float32)
    return jnp.broadcast_to(own[:, None], (rows, LANES))


def write_state(state, payload, field, extra):
    levels, rows, sector = state.shape[1:]
    width = payload.shape[-1]
    tail = sector - (width - LANES)
    payload[field, :, :, :width - LANES] = state[field, :, :, :width - LANES]
    end = jnp.concatenate([state[field, :, :, width - LANES:], extra[:, :, tail:]], axis=2)
    payload[field, :, :, width - LANES:] = end


def first_pack_kernel(adjoint, *refs):
    sources, (payload, state, rates, sems) = refs[:RATES], refs[RATES:]
    count, levels, rows, width = payload.shape
    sector = state.shape[-1]
    tail = sector - (width - LANES)
    copies = [pltpu.make_async_copy(adjoint.at[:count], state, sems.at[RATES])]
    for q, source in enumerate(sources):
        copies.append(pltpu.make_async_copy(source, rates.at[q], sems.at[q]))
    for copy in copies:
        copy.start()
    for copy in copies[1:]:
        copy.wait()
    lat = lax.axis_index("lat")
    top = jnp.where(lat == lax.axis_size("lat") - 1, rows - 1, rows)
    lane = lax.broadcasted_iota(jnp.int32, (levels, rows, LANES), 2)
    row = lax.broadcasted_iota(jnp.int32, (levels, rows, LANES), 1)
    edges = jnp.zeros((levels, rows, LANES), jnp.float32)
    for q in range(RATES):
        at = edge_lane(sector) + 2 * HALO * q
        head = pltpu.roll(rates[q, :, :, :LANES], at, 2)
        end = jnp.concatenate([rates[q, :, :, width - LANES:], jnp.zeros((levels, rows, LANES - tail), jnp.float32)], axis=2)
        end = pltpu.roll(end, (at + HALO - (tail - HALO)) % LANES, 2)
        if q == 0:
            head, end = jnp.where(row < top, head, 0.0), jnp.where(row < top, end, 0.0)
        edges = jnp.where((lane >= at) & (lane < at + HALO), head, edges)
        edges = jnp.where((lane >= at + HALO) & (lane < at + 2 * HALO), end, edges)
    copies[0].wait()
    zero = jnp.zeros((levels, rows, LANES), jnp.float32)
    for field in range(count):
        write_state(state, payload, field, edges if field == 0 else zero)


def rest_pack_kernel(chunks, adjoint, *refs):
    sources = refs[:RATES]
    count = len(chunks) - 1
    payloads = refs[RATES:RATES + count]
    own_out, first_out, second_out = refs[RATES + count:RATES + count + 3]
    state, rates, sems = refs[RATES + count + 3:]
    levels, rows, sector = sources[0].shape
    width = own_out.shape[-1]
    copies = [pltpu.make_async_copy(src, rates.at[q], sems.at[q]) for q, src in enumerate(sources)]
    if count:
        copies.append(pltpu.make_async_copy(adjoint.at[chunks[0]:], state, sems.at[RATES]))
    for copy in copies:
        copy.start()
    for copy in copies[:RATES]:
        copy.wait()
    lat = lax.axis_index("lat")
    is_last = lat == lax.axis_size("lat") - 1
    row = lax.broadcasted_iota(jnp.int32, (levels, rows, LANES), 1)
    for q in range(RATES):
        for start in range(0, width, LANES):
            size = min(LANES, sector - start)
            tile = rates[q, :, :, start:start + size]
            if size < LANES:
                tile = jnp.concatenate([tile, jnp.zeros((levels, rows, LANES - size), jnp.float32)], axis=2)
            if q == 0:
                tile = jnp.where(jnp.logical_and(is_last, row == rows - 1), 0.0, tile)
            own_out[:, q, :, start:start + LANES] = jnp.swapaxes(tile, 0, 1)
    if count:
        copies[RATES].wait()
    zero = jnp.zeros((levels, rows, LANES), jnp.float32)
    at = 0
    for c in range(count):
        for j in range(chunks[c + 1]):
            write_state(state.at[at:at + 1], payloads[c].at[j:j + 1], 0, zero)
            at += 1
    top = rows - HALO
    to_next = lax.rem(lat, 2) == 0

    @pl.when(to_next)
    def _():
        first_out[...] = own_out[top:]
        second_out[...] = own_out[:HALO]

    @pl.when(jnp.logical_not(to_next))
    def _():
        first_out[...] = own_out[:HALO]
        second_out[...] = own_out[top:]


def by_side(first_ref, second_ref, use):
    to_next = lax.rem(lax.axis_index("lat"), 2) == 0

    @pl.when(to_next)
    def _():
        use(second_ref, first_ref)

    @pl.when(jnp.logical_not(to_next))
    def _():
        use(first_ref, second_ref)


def coupling_power(coupling_ref):
    fields, levels, _ = coupling_ref.shape
    base = []
    for g in range(fields):
        line = coupling_ref[g]
        base.append([jnp.broadcast_to(line[:, f:f + 1], (levels, LANES)) for f in range(fields)])
        base[g][g] = base[g][g] + 1.0

    def product(left, right):
        def entry(g, f):
            return functools.reduce(jnp.add, [left[g][h] * right[h][f] for h in range(fields)])

        return [[entry(g, f) for f in range(fields)] for g in range(fields)]

    power = base
    for bit in bin(SUBSTEPS)[3:]:
        power = product(power, power)
        if bit == "1":
            power = product(power, base)
    return power


def face_kernel(sector, coupling, rate_own, rate_first, rate_second, own, first, second, level, power_out):
    power = coupling_power(coupling)
    for g, entries in enumerate(power):
        for f, value in enumerate(entries):
            power_out[g, f] = value
    rows, kinds, levels, width = rate_own.shape
    extent = rows + 2 * HALO
    tiles = width // LANES
    final = slice(width - LANES, width)
    lane = lax.broadcasted_iota(jnp.int32, (levels, LANES), 1)
    end = sector % LANES

    def extend(ref, edge_ref, base):
        count = ref.shape[0]
        for q in range(kinds):
            at = edge_lane(sector) + 2 * HALO * q
            edges = [edge_ref[0, r, :, final] for r in range(count)]
            ahead = [pltpu.roll(e, (end - at) % LANES, 1) for e in edges]
            behind = [pltpu.roll(e, (LANES - HALO - at - HALO) % LANES, 1) for e in edges]
            for r in range(count):
                piece = jnp.where((lane >= end) & (lane < end + HALO), ahead[r], ref[r, q, :, final])
                piece = jnp.where(lane >= LANES - HALO, behind[r], piece)
                level[base + r, q, :, :width - LANES] = ref[r, q, :, :width - LANES]
                level[base + r, q, :, final] = piece

    extend(rate_own, own, HALO)

    def halos(below, above, below_edges, above_edges):
        extend(below, below_edges, 0)
        extend(above, above_edges, HALO + rows)

    to_next = lax.rem(lax.axis_index("lat"), 2) == 0

    @pl.when(to_next)
    def _():
        halos(rate_second, rate_first, second, first)

    @pl.when(jnp.logical_not(to_next))
    def _():
        halos(rate_first, rate_second, first, second)

    for r in range(extent - 2, 0, -1):
        west = shifted([level[r, 3, :, t * LANES:(t + 1) * LANES] for t in range(tiles)], 1)
        for t in range(tiles):
            span = slice(t * LANES, (t + 1) * LANES)
            north, south, east = level[r, 0, :, span], level[r - 1, 1, :, span], level[r, 2, :, span]
            level[r, 1, :, span] = south
            level[r, 3, :, span] = west[t]
            level[r, 4, :, span] = 1.0 - east - west[t] - north - south


def shifted(tiles, step):
    lane = lax.broadcasted_iota(jnp.int32, tiles[0].shape, 1)
    rolled = [pltpu.roll(tile, step % LANES, 1) for tile in tiles]
    border = lane == (0 if step == 1 else LANES - 1)
    count = len(tiles)
    return [jnp.where(border, rolled[(t - step) % count], rolled[t]) for t in range(count)]


def transport_kernel(chunk, finished, sector, power_ref, rates, own_ref, first_ref, second_ref, *refs):
    earlier = refs[:finished]
    out_ref, even, odd, stage = refs[finished:]
    rows, levels, width = own_ref.shape[1:]
    extent = rows + 2 * HALO
    tiles = width // LANES
    last = finished > 0

    def put(ref, base):
        even[:, base:base + ref.shape[1]] = ref[...]

    put(own_ref, HALO)

    def halos(below, above):
        put(below, 0)
        put(above, HALO + rows)

    by_side(first_ref, second_ref, halos)

    def line(source, r, field):
        return [source[field, r, :, t * LANES:(t + 1) * LANES] for t in range(tiles)]

    for step in range(SUBSTEPS):
        source, target = (even, odd) if step % 2 == 0 else (odd, even)
        count = extent - 2 - 2 * step

        def finish(field, r, here, ahead, behind):
            for t in range(tiles):
                span = slice(t * LANES, (t + 1) * LANES)
                north, south, east, west, stay = (rates[r, q, :, span] for q in range(5))
                target[field, r, :, span] = (
                    (stay * here[t] + (north * source[field, r + 1, :, span] + south * source[field, r - 1, :, span]))
                    + (east * ahead[t] + west * behind[t])
                )

        def work(first, number, field):
            for r in [first + j for j in range(number)]:
                here = line(source, r, field)
                finish(field, r, here, shifted(here, -1), shifted(here, 1))

        for field in range(chunk):
            def group(index, carry):
                work(step + 1 + ROWS_AT_ONCE * index, ROWS_AT_ONCE, field)
                return carry

            groups, rest = count // ROWS_AT_ONCE, count % ROWS_AT_ONCE
            if groups > 1:
                lax.fori_loop(0, groups, group, 0)
            else:
                work(step + 1, groups * ROWS_AT_ONCE, field)
            work(step + 1 + groups * ROWS_AT_ONCE, rest, field)
    result = even if SUBSTEPS % 2 == 0 else odd

    if not last:
        out_ref[...] = result[:, HALO:HALO + rows]
        return
    sources = [(ref, j, 0) for ref in earlier for j in range(ref.shape[0])]
    sources += [(result, j, HALO) for j in range(chunk)]
    fields = len(sources)
    def mix(f, carry):
        for start in range(0, sector, LANES):
            stop = min(start + LANES, sector)
            for r in range(rows):
                terms = [power_ref[g, f] * ref[j, base + r, :, start:start + LANES]
                         for g, (ref, j, base) in enumerate(sources)]
                stage[start // LANES, r * levels:(r + 1) * levels] = functools.reduce(jnp.add, terms)
            for level in range(levels):
                value = stage[start // LANES, pl.ds(level, rows, stride=levels), :]
                out_ref[f, level, :, start:stop] = value[:, :stop - start]
        return carry

    lax.fori_loop(0, fields, mix, 0)


def lat_pairs(count):
    def both(start):
        ups = [(i, i + 1) for i in range(start, count - 1, 2)]
        return ups + [(j, i) for i, j in ups]

    return both(0), both(1)


def shards(adjoint_in, lat_ahead, lat_behind, lon_ahead, lon_behind, coupling, cutoff):
    fields, levels, rows, sector = adjoint_in.shape
    sectors = lax.axis_size("lon")
    length = sector * sectors
    width = -(-(sector + 2 * HALO) // LANES) * LANES
    even_pairs, odd_pairs = lat_pairs(lax.axis_size("lat"))
    f32 = jnp.float32
    chunks = CHUNKS if sum(CHUNKS) == fields else (fields,)

    def sector_ahead(values, offset):
        return lax.ppermute(values, "lon", [(s, (s - offset) % sectors) for s in range(sectors)])

    def to_bands(first, second):
        return lax.ppermute(first, "lat", even_pairs), lax.ppermute(second, "lat", odd_pairs)

    extent = rows + 2 * HALO
    rate_shape = (RATES, levels, width)
    inputs = [
        pltpu.with_memory_space_constraint(array, pltpu.HBM)
        for array in (adjoint_in, lat_ahead, lat_behind, lon_ahead, lon_behind)
    ]
    payload_shapes = [jax.ShapeDtypeStruct((n, levels, rows, width), f32) for n in chunks]
    later = max(fields - chunks[0], 1)
    first_payload = pl.pallas_call(
        first_pack_kernel,
        out_shape=payload_shapes[0],
        in_specs=[HBM] * (1 + RATES),
        out_specs=VMEM,
        scratch_shapes=[
            pltpu.VMEM((chunks[0],) + adjoint_in.shape[1:], f32),
            pltpu.VMEM((RATES,) + lat_ahead.shape, f32),
            pltpu.SemaphoreType.DMA((1 + RATES,)),
        ],
        compiler_params=PARAMS,
        name="first_pack",
    )(*inputs)
    first_circle = [first_payload] + [sector_ahead(first_payload, k) for k in range(1, sectors)]
    *payloads, rate_own, rate_first, rate_second = pl.pallas_call(
        functools.partial(rest_pack_kernel, chunks),
        out_shape=(
            *payload_shapes[1:],
            jax.ShapeDtypeStruct((rows,) + rate_shape, f32),
            jax.ShapeDtypeStruct((HALO,) + rate_shape, f32),
            jax.ShapeDtypeStruct((HALO,) + rate_shape, f32),
        ),
        in_specs=[HBM] * (1 + RATES),
        out_specs=(VMEM,) * (len(chunks) + 2),
        scratch_shapes=[
            pltpu.VMEM((later,) + adjoint_in.shape[1:], f32),
            pltpu.VMEM((RATES,) + lat_ahead.shape, f32),
            pltpu.SemaphoreType.DMA((1 + RATES,)),
        ],
        compiler_params=PARAMS,
        name="rest_pack",
    )(*inputs)
    circles = [[part] + [sector_ahead(part, k) for k in range(1, sectors)] for part in payloads]
    circles.insert(0, first_circle)
    rate_first, rate_second = to_bands(rate_first, rate_second)

    limits = limits_of(cutoff, rows)
    table = jnp.asarray(mode_tables(length))
    results = []
    for c, (n, circle) in enumerate(zip(chunks, circles)):
        lines = n * levels * rows
        own, first, second = pl.pallas_call(
            functools.partial(filter_kernel, sectors, c == 0),
            out_shape=(
                jax.ShapeDtypeStruct((n, rows, levels, width), f32),
                jax.ShapeDtypeStruct((n, HALO, levels, width), f32),
                jax.ShapeDtypeStruct((n, HALO, levels, width), f32),
            ),
            in_specs=[VMEM] * (sectors + 2),
            out_specs=(VMEM,) * 3,
            scratch_shapes=[
                pltpu.VMEM((length // LANES, lines, LANES), f32),
                pltpu.VMEM((length // LANES, lines, LANES), f32),
            ],
            compiler_params=PARAMS,
            name="polar_filter",
        )(limits, table, *circle)
        first, second = to_bands(first, second)
        if c == 0:
            level, power = pl.pallas_call(
                functools.partial(face_kernel, sector),
                out_shape=(
                    jax.ShapeDtypeStruct((extent, 5, levels, width), f32),
                    jax.ShapeDtypeStruct((fields, fields, levels, LANES), f32),
                ),
                in_specs=[VMEM] * 7,
                out_specs=(VMEM,) * 2,
                compiler_params=PARAMS,
                name="faces",
            )(jnp.transpose(coupling, (1, 0, 2)), rate_own, rate_first, rate_second, own, first, second)
        is_last = c == len(chunks) - 1
        earlier = results if is_last else []
        shape = adjoint_in.shape if is_last else (n, rows, levels, width)
        results.append(pl.pallas_call(
            functools.partial(transport_kernel, n, len(earlier), sector),
            out_shape=jax.ShapeDtypeStruct(shape, f32),
            in_specs=[VMEM] * (5 + len(earlier)),
            out_specs=VMEM,
            scratch_shapes=[
                pltpu.VMEM((n, extent, levels, width), f32),
                pltpu.VMEM((n, extent, levels, width), f32),
                pltpu.VMEM((width // LANES, rows * levels, LANES), f32),
            ],
            compiler_params=PARAMS,
            name="transport",
        )(power, level, own, first, second, *earlier))
    return results[-1]


def solution(mesh):
    placed = (
        P("member", "lev", "lat", "lon"),
        P(("member", "lev"), "lat", "lon"),
        P(("member", "lev"), "lat", "lon"),
        P(("member", "lev"), "lat", "lon"),
        P(("member", "lev"), "lat", "lon"),
        P("lev", None, None),
        P(),
    )
    return jax.shard_map(
        shards,
        mesh=mesh,
        in_specs=placed,
        out_specs=P("member", "lev", "lat", "lon"),
        check_vma=False,
    )
```

```python
import functools
import math

import jax
import jax.numpy as jnp
import numpy as np
from jax import lax
from jax.experimental import pallas as pl
from jax.experimental.pallas import tpu as pltpu
from jax.sharding import PartitionSpec as P

SUBSTEPS = 6
HALO = SUBSTEPS
LANES = 128
RATES = 4
CHUNKS = (3, 2)
ROWS_AT_ONCE = 9
PARAMS = pltpu.CompilerParams(vmem_limit_bytes=12 * 2**20)
VMEM = pl.BlockSpec(memory_space=pltpu.VMEM)
HBM = pl.BlockSpec(memory_space=pltpu.HBM)


def split_bf16(values):
    high = values.astype(jnp.bfloat16)
    low = (values - high.astype(jnp.float32)).astype(jnp.bfloat16)
    return high, low


def split_bf16_numpy(values):
    values = values.astype(np.float32)
    high = values.astype(jnp.bfloat16)
    low = (values - high.astype(np.float32)).astype(jnp.bfloat16)
    return high, low


def mode_tables(length):
    ways = length // LANES
    point = np.arange(LANES)[:, None].astype(np.int64)
    column = np.arange(LANES)[None, :].astype(np.int64)
    half = LANES // 2
    wave = np.where(column <= half, column, column - half)
    angle = 2.0 * np.pi * (point * wave % LANES) / LANES
    weight = np.where((column == 0) | (column == half), 1.0 / LANES, 2.0 / LANES)
    real_block = np.where(column <= half, np.cos(angle), np.sin(angle)) * np.sqrt(weight)
    blocks = []
    for first in range(1, (ways + 1) // 2):
        angle = 2.0 * np.pi * (point * (first + ways * column) % length) / length
        cosine, sine = np.cos(angle), np.sin(angle)
        blocks.append(np.block([[cosine, -sine], [sine, cosine]]) / math.sqrt(LANES))
    block_high, block_low = split_bf16_numpy(np.stack(blocks))
    real = np.zeros((1, 2 * LANES, 2 * LANES), block_high.dtype)
    real[0, :LANES, :LANES], real[0, :LANES, LANES:] = split_bf16_numpy(real_block)
    return np.concatenate([block_high, block_low, real])


def dot_split(values, high_table, low_table, transposed):
    dims = (((1,), (1 if transposed else 0,)), ((), ()))
    count = values.shape[0]
    high, low = split_bf16(values)
    dot = functools.partial(lax.dot_general, dimension_numbers=dims, preferred_element_type=jnp.float32)
    main = dot(jnp.concatenate([high, low], axis=0), high_table)
    return main[:count] + (main[count:] + dot(high, low_table))


def damping_of(limit, wavenumber):
    ratio = limit / jnp.maximum(wavenumber, 1.0)
    return jnp.where(wavenumber > limit, ratio * ratio, 1.0)


def filter_kernel(sectors, edges, limit_ref, table, *refs):
    circle_refs = refs[:sectors]
    own_out, first_out, second_out = refs[sectors:sectors + 3]
    wide, sums = refs[sectors + 3:]
    fields, levels, rows, width = circle_refs[0].shape
    ways = wide.shape[0]
    length = ways * LANES
    sector = length // sectors
    pairs = (ways - 1) // 2
    tiles = width // LANES
    per_field = levels * rows
    lat = lax.axis_index("lat")
    limit = limit_ref[...]

    lines = fields * per_field
    line_lane = lax.broadcasted_iota(jnp.int32, (lines, LANES), 1)
    rolled = {}

    def part(k, t):
        if (k, t) not in rolled:
            tile = circle_refs[k][:, :, :, t * LANES:(t + 1) * LANES].reshape(lines, LANES)
            offset = k * sector % LANES
            rolled[k, t] = pltpu.roll(tile, offset, 1) if offset else tile
        return rolled[k, t]

    def assemble(a):
        tile = None
        for k in range(sectors):
            low, high = k * sector, (k + 1) * sector
            if high <= a * LANES or low >= (a + 1) * LANES:
                continue
            t, offset = a - low // LANES, low % LANES
            here = part(k, t) if t * LANES < sector else part(k, t - 1)
            if offset and t > 0 and t * LANES < sector:
                here = jnp.where(line_lane < offset, part(k, t - 1), here)
            tile = here if tile is None else jnp.where(line_lane < low - a * LANES, tile, here)
        wide[a] = tile

    for a in range(ways):
        if a < tiles or a == ways - 1:
            assemble(a)

    @pl.when(jnp.min(limit) < length // 2)
    def _():
        rolled.clear()
        for a in range(tiles, ways - 1):
            assemble(a)
        lane = lax.broadcasted_iota(jnp.int32, (rows, LANES), 1)

        def damp(spectrum, damping):
            shaped = spectrum.reshape(fields * levels, rows, damping.shape[-1])
            return (shaped * damping[None]).reshape(spectrum.shape)

        folds = range(1, pairs + 1)
        wanted = [a for a in folds if a == 1 or a < tiles or ways - a < tiles]
        origin = wide[0]
        total = origin
        for a in folds:
            low, high = wide[a], wide[ways - a]
            wide[a], wide[ways - a] = low + high, low - high
            total = total + wide[a]
        half = LANES // 2
        wave = (jnp.where(lane <= half, lane, lane - half) * ways).astype(jnp.float32)
        real_high, real_low = table[2 * pairs, :LANES, :LANES], table[2 * pairs, :LANES, LANES:]
        spectrum = damp(dot_split(total, real_high, real_low, False), damping_of(limit, wave))
        base = dot_split(spectrum, real_high, real_low, True) * (1.0 / ways)
        for k in folds:
            turn = [2.0 * math.pi * (a * k % ways) / ways for a in folds]
            cosines = wide[0] + sum(math.cos(t) * wide[a] for t, a in zip(turn, folds))
            sines = -sum(math.sin(t) * wide[ways - a] for t, a in zip(turn, folds))
            mode = k + ways * lane
            one = damping_of(limit, jnp.minimum(mode, length - mode).astype(jnp.float32))
            damping = jnp.concatenate([one, one], axis=1) * (2.0 / ways)
            high, low = table[k - 1], table[pairs + k - 1]
            spectrum = dot_split(jnp.concatenate([cosines, sines], axis=1), high, low, False)
            wave_back = dot_split(damp(spectrum, damping), high, low, True)
            cosines, sines = wave_back[:, :LANES], wave_back[:, LANES:]
            sums[0] = (base if k == 1 else sums[0]) + cosines
            for a in wanted:
                t = 2.0 * math.pi * (a * k % ways) / ways
                sums[a] = (base if k == 1 else sums[a]) + math.cos(t) * cosines
                part_sines = math.sin(t) * sines
                sums[pairs + a] = part_sines if k == 1 else sums[pairs + a] + part_sines
        wide[0] = sums[0]
        for a in wanted:
            if a < tiles:
                wide[a] = sums[a] - sums[pairs + a]
            if a == 1 or ways - a < tiles:
                wide[ways - a] = sums[a] + sums[pairs + a]

    def emit(field, carry):
        lane = lax.broadcasted_iota(jnp.int32, (levels, LANES), 1)
        for r in range(rows):
            span = pl.ds(field * per_field + r, levels, stride=rows)
            for a in range(tiles):
                tile = wide[a, span, :]
                if a == tiles - 1:
                    behind = wide[ways - 1, span, :]
                    tile = jnp.where(lane >= LANES - HALO, behind, tile)
                own_out[field, r, :, a * LANES:(a + 1) * LANES] = tile
        return carry

    lax.fori_loop(0, fields, emit, 0)
    if edges:
        final = slice(width - LANES, width)
        ahead = jnp.swapaxes(circle_refs[1][0, :, :, final], 0, 1)
        behind = jnp.swapaxes(circle_refs[sectors - 1][0, :, :, final], 0, 1)
        first_lane = edge_lane(sector)
        lane = lax.broadcasted_iota(jnp.int32, (rows, levels, LANES), 2) - first_lane
        spare = jnp.where(lane % (2 * HALO) < HALO, ahead, behind)
        spare = jnp.where((lane >= 0) & (lane < RATES * 2 * HALO), spare, own_out[0, :, :, final])
        own_out[0, :, :, final] = spare

    top = rows - HALO
    to_next = lax.rem(lat, 2) == 0

    @pl.when(to_next)
    def _():
        first_out[...] = own_out[:, top:]
        second_out[...] = own_out[:, :HALO]

    @pl.when(jnp.logical_not(to_next))
    def _():
        first_out[...] = own_out[:, :HALO]
        second_out[...] = own_out[:, top:]


def edge_lane(sector):
    return sector % LANES + HALO


def write_state(state, payload, field, extra):
    levels, rows, sector = state.shape[1:]
    width = payload.shape[-1]
    tail = sector - (width - LANES)
    payload[field, :, :, :width - LANES] = state[field, :, :, :width - LANES]
    end = jnp.concatenate([state[field, :, :, width - LANES:], extra[:, :, tail:]], axis=2)
    payload[field, :, :, width - LANES:] = end


def first_pack_kernel(adjoint, *refs):
    sources, (payload, state, rates, sems) = refs[:RATES], refs[RATES:]
    count, levels, rows, width = payload.shape
    sector = state.shape[-1]
    tail = sector - (width - LANES)
    copies = [pltpu.make_async_copy(adjoint.at[:count], state, sems.at[RATES])]
    for q, source in enumerate(sources):
        copies.append(pltpu.make_async_copy(source, rates.at[q], sems.at[q]))
    for copy in copies:
        copy.start()
    for copy in copies[1:]:
        copy.wait()
    lat = lax.axis_index("lat")
    top = jnp.where(lat == lax.axis_size("lat") - 1, rows - 1, rows)
    lane = lax.broadcasted_iota(jnp.int32, (levels, rows, LANES), 2)
    row = lax.broadcasted_iota(jnp.int32, (levels, rows, LANES), 1)
    edges = jnp.zeros((levels, rows, LANES), jnp.float32)
    for q in range(RATES):
        at = edge_lane(sector) + 2 * HALO * q
        head = pltpu.roll(rates[q, :, :, :LANES], at, 2)
        end = jnp.concatenate([rates[q, :, :, width - LANES:], jnp.zeros((levels, rows, LANES - tail), jnp.float32)], axis=2)
        end = pltpu.roll(end, (at + HALO - (tail - HALO)) % LANES, 2)
        if q == 0:
            head, end = jnp.where(row < top, head, 0.0), jnp.where(row < top, end, 0.0)
        edges = jnp.where((lane >= at) & (lane < at + HALO), head, edges)
        edges = jnp.where((lane >= at + HALO) & (lane < at + 2 * HALO), end, edges)
    copies[0].wait()
    zero = jnp.zeros((levels, rows, LANES), jnp.float32)
    for field in range(count):
        write_state(state, payload, field, edges if field == 0 else zero)


def rest_pack_kernel(chunks, cutoff, adjoint, *refs):
    sources = refs[:RATES]
    count = len(chunks) - 1
    payloads = refs[RATES:RATES + count]
    own_out, first_out, second_out, limit_out = refs[RATES + count:RATES + count + 4]
    state, rates, cutoffs, sems = refs[RATES + count + 4:]
    levels, rows, sector = sources[0].shape
    width = own_out.shape[-1]
    cutoff_copy = pltpu.make_async_copy(cutoff, cutoffs, sems.at[RATES + 1])
    cutoff_copy.start()
    copies = [pltpu.make_async_copy(src, rates.at[q], sems.at[q]) for q, src in enumerate(sources)]
    if count:
        copies.append(pltpu.make_async_copy(adjoint.at[chunks[0]:], state, sems.at[RATES]))
    for copy in copies:
        copy.start()
    for copy in copies[:RATES]:
        copy.wait()
    lat = lax.axis_index("lat")
    is_last = lat == lax.axis_size("lat") - 1
    row = lax.broadcasted_iota(jnp.int32, (levels, rows, LANES), 1)
    for q in range(RATES):
        for start in range(0, width, LANES):
            size = min(LANES, sector - start)
            tile = rates[q, :, :, start:start + size]
            if size < LANES:
                tile = jnp.concatenate([tile, jnp.zeros((levels, rows, LANES - size), jnp.float32)], axis=2)
            if q == 0:
                tile = jnp.where(jnp.logical_and(is_last, row == rows - 1), 0.0, tile)
            own_out[:, q, :, start:start + LANES] = jnp.swapaxes(tile, 0, 1)
    cutoff_copy.wait()
    sublane = lax.broadcasted_iota(jnp.int32, (rows, LANES), 0)
    limit = jnp.zeros((rows, LANES), jnp.float32)
    for j in range(rows):
        limit = jnp.where(sublane == j, cutoffs[lat * rows + j].astype(jnp.float32), limit)
    limit_out[...] = limit
    if count:
        copies[RATES].wait()
    zero = jnp.zeros((levels, rows, LANES), jnp.float32)
    at = 0
    for c in range(count):
        for j in range(chunks[c + 1]):
            write_state(state.at[at:at + 1], payloads[c].at[j:j + 1], 0, zero)
            at += 1
    top = rows - HALO
    to_next = lax.rem(lat, 2) == 0

    @pl.when(to_next)
    def _():
        first_out[...] = own_out[top:]
        second_out[...] = own_out[:HALO]

    @pl.when(jnp.logical_not(to_next))
    def _():
        first_out[...] = own_out[:HALO]
        second_out[...] = own_out[top:]


def by_side(first_ref, second_ref, use):
    to_next = lax.rem(lax.axis_index("lat"), 2) == 0

    @pl.when(to_next)
    def _():
        use(second_ref, first_ref)

    @pl.when(jnp.logical_not(to_next))
    def _():
        use(first_ref, second_ref)


def coupling_power(coupling_ref):
    fields, levels, _ = coupling_ref.shape
    base = []
    for g in range(fields):
        line = coupling_ref[g]
        base.append([jnp.broadcast_to(line[:, f:f + 1], (levels, LANES)) for f in range(fields)])
        base[g][g] = base[g][g] + 1.0

    def product(left, right):
        def entry(g, f):
            return functools.reduce(jnp.add, [left[g][h] * right[h][f] for h in range(fields)])

        return [[entry(g, f) for f in range(fields)] for g in range(fields)]

    power = base
    for bit in bin(SUBSTEPS)[3:]:
        power = product(power, power)
        if bit == "1":
            power = product(power, base)
    return power


def face_kernel(sector, coupling, rate_own, rate_first, rate_second, own, first, second, level, power_out):
    power = coupling_power(coupling)
    for g, entries in enumerate(power):
        for f, value in enumerate(entries):
            power_out[g, f] = value
    rows, kinds, levels, width = rate_own.shape
    extent = rows + 2 * HALO
    tiles = width // LANES
    final = slice(width - LANES, width)
    lane = lax.broadcasted_iota(jnp.int32, (levels, LANES), 1)
    end = sector % LANES

    def extend(ref, edge_ref, base):
        count = ref.shape[0]
        for q in range(kinds):
            at = edge_lane(sector) + 2 * HALO * q
            edges = [edge_ref[0, r, :, final] for r in range(count)]
            ahead = [pltpu.roll(e, (end - at) % LANES, 1) for e in edges]
            behind = [pltpu.roll(e, (LANES - HALO - at - HALO) % LANES, 1) for e in edges]
            for r in range(count):
                piece = jnp.where((lane >= end) & (lane < end + HALO), ahead[r], ref[r, q, :, final])
                piece = jnp.where(lane >= LANES - HALO, behind[r], piece)
                level[base + r, q, :, :width - LANES] = ref[r, q, :, :width - LANES]
                level[base + r, q, :, final] = piece

    extend(rate_own, own, HALO)

    def halos(below, above, below_edges, above_edges):
        extend(below, below_edges, 0)
        extend(above, above_edges, HALO + rows)

    to_next = lax.rem(lax.axis_index("lat"), 2) == 0

    @pl.when(to_next)
    def _():
        halos(rate_second, rate_first, second, first)

    @pl.when(jnp.logical_not(to_next))
    def _():
        halos(rate_first, rate_second, first, second)

    for r in range(extent - 2, 0, -1):
        west = shifted([level[r, 3, :, t * LANES:(t + 1) * LANES] for t in range(tiles)], 1)
        for t in range(tiles):
            span = slice(t * LANES, (t + 1) * LANES)
            north, south, east = level[r, 0, :, span], level[r - 1, 1, :, span], level[r, 2, :, span]
            level[r, 1, :, span] = south
            level[r, 3, :, span] = west[t]
            level[r, 4, :, span] = 1.0 - east - west[t] - north - south


def shifted(tiles, step):
    lane = lax.broadcasted_iota(jnp.int32, tiles[0].shape, 1)
    rolled = [pltpu.roll(tile, step % LANES, 1) for tile in tiles]
    border = lane == (0 if step == 1 else LANES - 1)
    count = len(tiles)
    return [jnp.where(border, rolled[(t - step) % count], rolled[t]) for t in range(count)]


def transport_kernel(chunk, finished, sector, power_ref, rates, own_ref, first_ref, second_ref, *refs):
    earlier = refs[:finished]
    out_ref, even, odd, stage = refs[finished:]
    rows, levels, width = own_ref.shape[1:]
    extent = rows + 2 * HALO
    tiles = width // LANES
    last = finished > 0

    def put(ref, base):
        even[:, base:base + ref.shape[1]] = ref[...]

    put(own_ref, HALO)

    def halos(below, above):
        put(below, 0)
        put(above, HALO + rows)

    by_side(first_ref, second_ref, halos)

    def line(source, r, field):
        return [source[field, r, :, t * LANES:(t + 1) * LANES] for t in range(tiles)]

    for step in range(SUBSTEPS):
        source, target = (even, odd) if step % 2 == 0 else (odd, even)
        count = extent - 2 - 2 * step

        def finish(field, r, here, ahead, behind):
            for t in range(tiles):
                span = slice(t * LANES, (t + 1) * LANES)
                north, south, east, west, stay = (rates[r, q, :, span] for q in range(5))
                target[field, r, :, span] = (
                    (stay * here[t] + (north * source[field, r + 1, :, span] + south * source[field, r - 1, :, span]))
                    + (east * ahead[t] + west * behind[t])
                )

        def work(first, number, field):
            for r in [first + j for j in range(number)]:
                here = line(source, r, field)
                finish(field, r, here, shifted(here, -1), shifted(here, 1))

        for field in range(chunk):
            def group(index, carry):
                work(step + 1 + ROWS_AT_ONCE * index, ROWS_AT_ONCE, field)
                return carry

            groups, rest = count // ROWS_AT_ONCE, count % ROWS_AT_ONCE
            if groups > 1:
                lax.fori_loop(0, groups, group, 0)
            else:
                work(step + 1, groups * ROWS_AT_ONCE, field)
            work(step + 1 + groups * ROWS_AT_ONCE, rest, field)
    result = even if SUBSTEPS % 2 == 0 else odd

    if not last:
        out_ref[...] = result[:, HALO:HALO + rows]
        return
    sources = [(ref, j, 0) for ref in earlier for j in range(ref.shape[0])]
    sources += [(result, j, HALO) for j in range(chunk)]
    fields = len(sources)
    def mix(f, carry):
        for start in range(0, sector, LANES):
            stop = min(start + LANES, sector)
            for r in range(rows):
                terms = [power_ref[g, f] * ref[j, base + r, :, start:start + LANES]
                         for g, (ref, j, base) in enumerate(sources)]
                stage[start // LANES, r * levels:(r + 1) * levels] = functools.reduce(jnp.add, terms)
            for level in range(levels):
                value = stage[start // LANES, pl.ds(level, rows, stride=levels), :]
                out_ref[f, level, :, start:stop] = value[:, :stop - start]
        return carry

    lax.fori_loop(0, fields, mix, 0)


def lat_pairs(count):
    def both(start):
        ups = [(i, i + 1) for i in range(start, count - 1, 2)]
        return ups + [(j, i) for i, j in ups]

    return both(0), both(1)


def shards(adjoint_in, lat_ahead, lat_behind, lon_ahead, lon_behind, coupling, cutoff):
    fields, levels, rows, sector = adjoint_in.shape
    sectors = lax.axis_size("lon")
    length = sector * sectors
    width = -(-(sector + 2 * HALO) // LANES) * LANES
    even_pairs, odd_pairs = lat_pairs(lax.axis_size("lat"))
    f32 = jnp.float32
    chunks = CHUNKS if sum(CHUNKS) == fields else (fields,)

    def sector_ahead(values, offset):
        return lax.ppermute(values, "lon", [(s, (s - offset) % sectors) for s in range(sectors)])

    def to_bands(first, second):
        return lax.ppermute(first, "lat", even_pairs), lax.ppermute(second, "lat", odd_pairs)

    extent = rows + 2 * HALO
    rate_shape = (RATES, levels, width)
    inputs = [
        pltpu.with_memory_space_constraint(array, pltpu.HBM)
        for array in (adjoint_in, lat_ahead, lat_behind, lon_ahead, lon_behind)
    ]
    payload_shapes = [jax.ShapeDtypeStruct((n, levels, rows, width), f32) for n in chunks]
    later = max(fields - chunks[0], 1)
    first_payload = pl.pallas_call(
        first_pack_kernel,
        out_shape=payload_shapes[0],
        in_specs=[HBM] * (1 + RATES),
        out_specs=VMEM,
        scratch_shapes=[
            pltpu.VMEM((chunks[0],) + adjoint_in.shape[1:], f32),
            pltpu.VMEM((RATES,) + lat_ahead.shape, f32),
            pltpu.SemaphoreType.DMA((1 + RATES,)),
        ],
        compiler_params=PARAMS,
        name="first_pack",
    )(*inputs)
    first_circle = [first_payload] + [sector_ahead(first_payload, k) for k in range(1, sectors)]
    *payloads, rate_own, rate_first, rate_second, limits = pl.pallas_call(
        functools.partial(rest_pack_kernel, chunks),
        out_shape=(
            *payload_shapes[1:],
            jax.ShapeDtypeStruct((rows,) + rate_shape, f32),
            jax.ShapeDtypeStruct((HALO,) + rate_shape, f32),
            jax.ShapeDtypeStruct((HALO,) + rate_shape, f32),
            jax.ShapeDtypeStruct((rows, LANES), f32),
        ),
        in_specs=[HBM] * (2 + RATES),
        out_specs=(VMEM,) * (len(chunks) + 3),
        scratch_shapes=[
            pltpu.VMEM((later,) + adjoint_in.shape[1:], f32),
            pltpu.VMEM((RATES,) + lat_ahead.shape, f32),
            pltpu.SMEM(cutoff.shape, cutoff.dtype),
            pltpu.SemaphoreType.DMA((2 + RATES,)),
        ],
        compiler_params=PARAMS,
        name="rest_pack",
    )(pltpu.with_memory_space_constraint(cutoff, pltpu.HBM), *inputs)
    circles = [[part] + [sector_ahead(part, k) for k in range(1, sectors)] for part in payloads]
    circles.insert(0, first_circle)
    rate_first, rate_second = to_bands(rate_first, rate_second)

    table = jnp.asarray(mode_tables(length))
    results = []
    for c, (n, circle) in enumerate(zip(chunks, circles)):
        lines = n * levels * rows
        own, first, second = pl.pallas_call(
            functools.partial(filter_kernel, sectors, c == 0),
            out_shape=(
                jax.ShapeDtypeStruct((n, rows, levels, width), f32),
                jax.ShapeDtypeStruct((n, HALO, levels, width), f32),
                jax.ShapeDtypeStruct((n, HALO, levels, width), f32),
            ),
            in_specs=[VMEM] * (sectors + 2),
            out_specs=(VMEM,) * 3,
            scratch_shapes=[
                pltpu.VMEM((length // LANES, lines, LANES), f32),
                pltpu.VMEM((length // LANES, lines, LANES), f32),
            ],
            compiler_params=PARAMS,
            name="polar_filter",
        )(limits, table, *circle)
        first, second = to_bands(first, second)
        if c == 0:
            level, power = pl.pallas_call(
                functools.partial(face_kernel, sector),
                out_shape=(
                    jax.ShapeDtypeStruct((extent, 5, levels, width), f32),
                    jax.ShapeDtypeStruct((fields, fields, levels, LANES), f32),
                ),
                in_specs=[VMEM] * 7,
                out_specs=(VMEM,) * 2,
                compiler_params=PARAMS,
                name="faces",
            )(jnp.transpose(coupling, (1, 0, 2)), rate_own, rate_first, rate_second, own, first, second)
        is_last = c == len(chunks) - 1
        earlier = results if is_last else []
        shape = adjoint_in.shape if is_last else (n, rows, levels, width)
        results.append(pl.pallas_call(
            functools.partial(transport_kernel, n, len(earlier), sector),
            out_shape=jax.ShapeDtypeStruct(shape, f32),
            in_specs=[VMEM] * (5 + len(earlier)),
            out_specs=VMEM,
            scratch_shapes=[
                pltpu.VMEM((n, extent, levels, width), f32),
                pltpu.VMEM((n, extent, levels, width), f32),
                pltpu.VMEM((width // LANES, rows * levels, LANES), f32),
            ],
            compiler_params=PARAMS,
            name="transport",
        )(power, level, own, first, second, *earlier))
    return results[-1]


def solution(mesh):
    placed = (
        P("member", "lev", "lat", "lon"),
        P(("member", "lev"), "lat", "lon"),
        P(("member", "lev"), "lat", "lon"),
        P(("member", "lev"), "lat", "lon"),
        P(("member", "lev"), "lat", "lon"),
        P("lev", None, None),
        P(),
    )
    return jax.shard_map(
        shards,
        mesh=mesh,
        in_specs=placed,
        out_specs=P("member", "lev", "lat", "lon"),
        check_vma=False,
    )
```

```python
import functools
import math

import jax
import jax.numpy as jnp
import numpy as np
from jax import lax
from jax.experimental import pallas as pl
from jax.experimental.pallas import tpu as pltpu
from jax.sharding import PartitionSpec as P

SUBSTEPS = 6
HALO = SUBSTEPS
LANES = 128
RATES = 4
CHUNKS = (3, 2)
ROWS_AT_ONCE = 9
PARAMS = pltpu.CompilerParams(vmem_limit_bytes=12 * 2**20)
VMEM = pl.BlockSpec(memory_space=pltpu.VMEM)
HBM = pl.BlockSpec(memory_space=pltpu.HBM)


def split_bf16(values):
    high = values.astype(jnp.bfloat16)
    low = (values - high.astype(jnp.float32)).astype(jnp.bfloat16)
    return high, low


def split_bf16_numpy(values):
    values = values.astype(np.float32)
    high = values.astype(jnp.bfloat16)
    low = (values - high.astype(np.float32)).astype(jnp.bfloat16)
    return high, low


def mode_tables(length):
    ways = length // LANES
    point = np.arange(LANES)[:, None].astype(np.int64)
    column = np.arange(LANES)[None, :].astype(np.int64)
    half = LANES // 2
    wave = np.where(column <= half, column, column - half)
    angle = 2.0 * np.pi * (point * wave % LANES) / LANES
    weight = np.where((column == 0) | (column == half), 1.0 / LANES, 2.0 / LANES)
    real_block = np.where(column <= half, np.cos(angle), np.sin(angle)) * np.sqrt(weight)
    blocks = []
    for first in range(1, (ways + 1) // 2):
        angle = 2.0 * np.pi * (point * (first + ways * column) % length) / length
        cosine, sine = np.cos(angle), np.sin(angle)
        blocks.append(np.block([[cosine, -sine], [sine, cosine]]) / math.sqrt(LANES))
    block_high, block_low = split_bf16_numpy(np.stack(blocks))
    real = np.zeros((1, 2 * LANES, 2 * LANES), block_high.dtype)
    real[0, :LANES, :LANES], real[0, :LANES, LANES:] = split_bf16_numpy(real_block)
    return np.concatenate([block_high, block_low, real])


def dot_split(values, high_table, low_table, transposed):
    dims = (((1,), (1 if transposed else 0,)), ((), ()))
    count = values.shape[0]
    high, low = split_bf16(values)
    dot = functools.partial(lax.dot_general, dimension_numbers=dims, preferred_element_type=jnp.float32)
    main = dot(jnp.concatenate([high, low], axis=0), high_table)
    return main[:count] + (main[count:] + dot(high, low_table))


def damping_of(limit, wavenumber):
    ratio = limit / jnp.maximum(wavenumber, 1.0)
    return jnp.where(wavenumber > limit, ratio * ratio, 1.0)


def filter_kernel(sectors, edges, powered, limit_ref, table, *refs):
    if powered:
        coupling, *refs = refs
        power_out = refs.pop(sectors + 3)
        for g, entries in enumerate(coupling_power(coupling)):
            for f, value in enumerate(entries):
                power_out[g, f] = value
    circle_refs = refs[:sectors]
    own_out, first_out, second_out = refs[sectors:sectors + 3]
    wide, sums = refs[sectors + 3:]
    fields, levels, rows, width = circle_refs[0].shape
    ways = wide.shape[0]
    length = ways * LANES
    sector = length // sectors
    pairs = (ways - 1) // 2
    tiles = width // LANES
    per_field = levels * rows
    lat = lax.axis_index("lat")
    limit = limit_ref[...]

    lines = fields * per_field
    line_lane = lax.broadcasted_iota(jnp.int32, (lines, LANES), 1)
    rolled = {}

    def part(k, t):
        if (k, t) not in rolled:
            tile = circle_refs[k][:, :, :, t * LANES:(t + 1) * LANES].reshape(lines, LANES)
            offset = k * sector % LANES
            rolled[k, t] = pltpu.roll(tile, offset, 1) if offset else tile
        return rolled[k, t]

    def assemble(a):
        tile = None
        for k in range(sectors):
            low, high = k * sector, (k + 1) * sector
            if high <= a * LANES or low >= (a + 1) * LANES:
                continue
            t, offset = a - low // LANES, low % LANES
            here = part(k, t) if t * LANES < sector else part(k, t - 1)
            if offset and t > 0 and t * LANES < sector:
                here = jnp.where(line_lane < offset, part(k, t - 1), here)
            tile = here if tile is None else jnp.where(line_lane < low - a * LANES, tile, here)
        wide[a] = tile

    for a in range(ways):
        if a < tiles or a == ways - 1:
            assemble(a)

    @pl.when(jnp.min(limit) < length // 2)
    def _():
        rolled.clear()
        for a in range(tiles, ways - 1):
            assemble(a)
        lane = lax.broadcasted_iota(jnp.int32, (rows, LANES), 1)

        def damp(spectrum, damping):
            shaped = spectrum.reshape(fields * levels, rows, damping.shape[-1])
            return (shaped * damping[None]).reshape(spectrum.shape)

        folds = range(1, pairs + 1)
        wanted = [a for a in folds if a == 1 or a < tiles or ways - a < tiles]
        origin = wide[0]
        total = origin
        for a in folds:
            low, high = wide[a], wide[ways - a]
            wide[a], wide[ways - a] = low + high, low - high
            total = total + wide[a]
        half = LANES // 2
        wave = (jnp.where(lane <= half, lane, lane - half) * ways).astype(jnp.float32)
        real_high, real_low = table[2 * pairs, :LANES, :LANES], table[2 * pairs, :LANES, LANES:]
        spectrum = damp(dot_split(total, real_high, real_low, False), damping_of(limit, wave))
        base = dot_split(spectrum, real_high, real_low, True) * (1.0 / ways)
        for k in folds:
            turn = [2.0 * math.pi * (a * k % ways) / ways for a in folds]
            cosines = wide[0] + sum(math.cos(t) * wide[a] for t, a in zip(turn, folds))
            sines = -sum(math.sin(t) * wide[ways - a] for t, a in zip(turn, folds))
            mode = k + ways * lane
            one = damping_of(limit, jnp.minimum(mode, length - mode).astype(jnp.float32))
            damping = jnp.concatenate([one, one], axis=1) * (2.0 / ways)
            high, low = table[k - 1], table[pairs + k - 1]
            spectrum = dot_split(jnp.concatenate([cosines, sines], axis=1), high, low, False)
            wave_back = dot_split(damp(spectrum, damping), high, low, True)
            cosines, sines = wave_back[:, :LANES], wave_back[:, LANES:]
            sums[0] = (base if k == 1 else sums[0]) + cosines
            for a in wanted:
                t = 2.0 * math.pi * (a * k % ways) / ways
                sums[a] = (base if k == 1 else sums[a]) + math.cos(t) * cosines
                part_sines = math.sin(t) * sines
                sums[pairs + a] = part_sines if k == 1 else sums[pairs + a] + part_sines
        wide[0] = sums[0]
        for a in wanted:
            if a < tiles:
                wide[a] = sums[a] - sums[pairs + a]
            if a == 1 or ways - a < tiles:
                wide[ways - a] = sums[a] + sums[pairs + a]

    def emit(field, carry):
        lane = lax.broadcasted_iota(jnp.int32, (levels, LANES), 1)
        for r in range(rows):
            span = pl.ds(field * per_field + r, levels, stride=rows)
            for a in range(tiles):
                tile = wide[a, span, :]
                if a == tiles - 1:
                    behind = wide[ways - 1, span, :]
                    tile = jnp.where(lane >= LANES - HALO, behind, tile)
                own_out[field, r, :, a * LANES:(a + 1) * LANES] = tile
        return carry

    lax.fori_loop(0, fields, emit, 0)
    if edges:
        final = slice(width - LANES, width)
        ahead = jnp.swapaxes(circle_refs[1][0, :, :, final], 0, 1)
        behind = jnp.swapaxes(circle_refs[sectors - 1][0, :, :, final], 0, 1)
        first_lane = edge_lane(sector)
        lane = lax.broadcasted_iota(jnp.int32, (rows, levels, LANES), 2) - first_lane
        spare = jnp.where(lane % (2 * HALO) < HALO, ahead, behind)
        spare = jnp.where((lane >= 0) & (lane < RATES * 2 * HALO), spare, own_out[0, :, :, final])
        own_out[0, :, :, final] = spare

    top = rows - HALO
    to_next = lax.rem(lat, 2) == 0

    @pl.when(to_next)
    def _():
        first_out[...] = own_out[:, top:]
        second_out[...] = own_out[:, :HALO]

    @pl.when(jnp.logical_not(to_next))
    def _():
        first_out[...] = own_out[:, :HALO]
        second_out[...] = own_out[:, top:]


def edge_lane(sector):
    return sector % LANES + HALO


def write_state(state, payload, field, extra):
    levels, rows, sector = state.shape[1:]
    width = payload.shape[-1]
    tail = sector - (width - LANES)
    payload[field, :, :, :width - LANES] = state[field, :, :, :width - LANES]
    end = jnp.concatenate([state[field, :, :, width - LANES:], extra[:, :, tail:]], axis=2)
    payload[field, :, :, width - LANES:] = end


def first_pack_kernel(adjoint, *refs):
    sources, (payload, state, rates, sems) = refs[:RATES], refs[RATES:]
    count, levels, rows, width = payload.shape
    sector = state.shape[-1]
    tail = sector - (width - LANES)
    copies = [pltpu.make_async_copy(adjoint.at[:count], state, sems.at[RATES])]
    for q, source in enumerate(sources):
        copies.append(pltpu.make_async_copy(source, rates.at[q], sems.at[q]))
    for copy in copies:
        copy.start()
    for copy in copies[1:]:
        copy.wait()
    lat = lax.axis_index("lat")
    top = jnp.where(lat == lax.axis_size("lat") - 1, rows - 1, rows)
    lane = lax.broadcasted_iota(jnp.int32, (levels, rows, LANES), 2)
    row = lax.broadcasted_iota(jnp.int32, (levels, rows, LANES), 1)
    edges = jnp.zeros((levels, rows, LANES), jnp.float32)
    for q in range(RATES):
        at = edge_lane(sector) + 2 * HALO * q
        head = pltpu.roll(rates[q, :, :, :LANES], at, 2)
        end = jnp.concatenate([rates[q, :, :, width - LANES:], jnp.zeros((levels, rows, LANES - tail), jnp.float32)], axis=2)
        end = pltpu.roll(end, (at + HALO - (tail - HALO)) % LANES, 2)
        if q == 0:
            head, end = jnp.where(row < top, head, 0.0), jnp.where(row < top, end, 0.0)
        edges = jnp.where((lane >= at) & (lane < at + HALO), head, edges)
        edges = jnp.where((lane >= at + HALO) & (lane < at + 2 * HALO), end, edges)
    copies[0].wait()
    zero = jnp.zeros((levels, rows, LANES), jnp.float32)
    for field in range(count):
        write_state(state, payload, field, edges if field == 0 else zero)


def rest_pack_kernel(chunks, cutoff, adjoint, *refs):
    sources = refs[:RATES]
    count = len(chunks) - 1
    payloads = refs[RATES:RATES + count]
    own_out, first_out, second_out, limit_out = refs[RATES + count:RATES + count + 4]
    state, rates, cutoffs, sems = refs[RATES + count + 4:]
    levels, rows, sector = sources[0].shape
    width = own_out.shape[-1]
    cutoff_copy = pltpu.make_async_copy(cutoff, cutoffs, sems.at[RATES + 1])
    cutoff_copy.start()
    copies = [pltpu.make_async_copy(src, rates.at[q], sems.at[q]) for q, src in enumerate(sources)]
    if count:
        copies.append(pltpu.make_async_copy(adjoint.at[chunks[0]:], state, sems.at[RATES]))
    for copy in copies:
        copy.start()
    for copy in copies[:RATES]:
        copy.wait()
    lat = lax.axis_index("lat")
    is_last = lat == lax.axis_size("lat") - 1
    row = lax.broadcasted_iota(jnp.int32, (levels, rows, LANES), 1)
    for q in range(RATES):
        for start in range(0, width, LANES):
            size = min(LANES, sector - start)
            tile = rates[q, :, :, start:start + size]
            if size < LANES:
                tile = jnp.concatenate([tile, jnp.zeros((levels, rows, LANES - size), jnp.float32)], axis=2)
            if q == 0:
                tile = jnp.where(jnp.logical_and(is_last, row == rows - 1), 0.0, tile)
            own_out[:, q, :, start:start + LANES] = jnp.swapaxes(tile, 0, 1)
    cutoff_copy.wait()
    sublane = lax.broadcasted_iota(jnp.int32, (rows, LANES), 0)
    limit = jnp.zeros((rows, LANES), jnp.float32)
    for j in range(rows):
        limit = jnp.where(sublane == j, cutoffs[lat * rows + j].astype(jnp.float32), limit)
    limit_out[...] = limit
    if count:
        copies[RATES].wait()
    zero = jnp.zeros((levels, rows, LANES), jnp.float32)
    at = 0
    for c in range(count):
        for j in range(chunks[c + 1]):
            write_state(state.at[at:at + 1], payloads[c].at[j:j + 1], 0, zero)
            at += 1
    top = rows - HALO
    to_next = lax.rem(lat, 2) == 0

    @pl.when(to_next)
    def _():
        first_out[...] = own_out[top:]
        second_out[...] = own_out[:HALO]

    @pl.when(jnp.logical_not(to_next))
    def _():
        first_out[...] = own_out[:HALO]
        second_out[...] = own_out[top:]


def by_side(first_ref, second_ref, use):
    to_next = lax.rem(lax.axis_index("lat"), 2) == 0

    @pl.when(to_next)
    def _():
        use(second_ref, first_ref)

    @pl.when(jnp.logical_not(to_next))
    def _():
        use(first_ref, second_ref)


def coupling_power(coupling_ref):
    fields, levels, _ = coupling_ref.shape
    base = []
    for g in range(fields):
        line = coupling_ref[g]
        base.append([jnp.broadcast_to(line[:, f:f + 1], (levels, LANES)) for f in range(fields)])
        base[g][g] = base[g][g] + 1.0

    def product(left, right):
        def entry(g, f):
            return functools.reduce(jnp.add, [left[g][h] * right[h][f] for h in range(fields)])

        return [[entry(g, f) for f in range(fields)] for g in range(fields)]

    power = base
    for bit in bin(SUBSTEPS)[3:]:
        power = product(power, power)
        if bit == "1":
            power = product(power, base)
    return power


def face_kernel(sector, rate_own, rate_first, rate_second, own, first, second, level):
    rows, kinds, levels, width = rate_own.shape
    extent = rows + 2 * HALO
    tiles = width // LANES
    final = slice(width - LANES, width)
    lane = lax.broadcasted_iota(jnp.int32, (levels, LANES), 1)
    end = sector % LANES

    def extend(ref, edge_ref, base):
        count = ref.shape[0]
        for q in range(kinds):
            at = edge_lane(sector) + 2 * HALO * q
            edges = [edge_ref[0, r, :, final] for r in range(count)]
            ahead = [pltpu.roll(e, (end - at) % LANES, 1) for e in edges]
            behind = [pltpu.roll(e, (LANES - HALO - at - HALO) % LANES, 1) for e in edges]
            for r in range(count):
                piece = jnp.where((lane >= end) & (lane < end + HALO), ahead[r], ref[r, q, :, final])
                piece = jnp.where(lane >= LANES - HALO, behind[r], piece)
                level[base + r, q, :, :width - LANES] = ref[r, q, :, :width - LANES]
                level[base + r, q, :, final] = piece

    extend(rate_own, own, HALO)

    def halos(below, above, below_edges, above_edges):
        extend(below, below_edges, 0)
        extend(above, above_edges, HALO + rows)

    to_next = lax.rem(lax.axis_index("lat"), 2) == 0

    @pl.when(to_next)
    def _():
        halos(rate_second, rate_first, second, first)

    @pl.when(jnp.logical_not(to_next))
    def _():
        halos(rate_first, rate_second, first, second)

    for r in range(extent - 2, 0, -1):
        west = shifted([level[r, 3, :, t * LANES:(t + 1) * LANES] for t in range(tiles)], 1)
        for t in range(tiles):
            span = slice(t * LANES, (t + 1) * LANES)
            north, south, east = level[r, 0, :, span], level[r - 1, 1, :, span], level[r, 2, :, span]
            level[r, 1, :, span] = south
            level[r, 3, :, span] = west[t]
            level[r, 4, :, span] = 1.0 - east - west[t] - north - south


def shifted(tiles, step):
    lane = lax.broadcasted_iota(jnp.int32, tiles[0].shape, 1)
    rolled = [pltpu.roll(tile, step % LANES, 1) for tile in tiles]
    border = lane == (0 if step == 1 else LANES - 1)
    count = len(tiles)
    return [jnp.where(border, rolled[(t - step) % count], rolled[t]) for t in range(count)]


def transport_kernel(chunk, finished, sector, power_ref, rates, own_ref, first_ref, second_ref, *refs):
    earlier = refs[:finished]
    out_ref, even, odd, stage = refs[finished:]
    rows, levels, width = own_ref.shape[1:]
    extent = rows + 2 * HALO
    tiles = width // LANES
    last = finished > 0

    def put(ref, base):
        even[:, base:base + ref.shape[1]] = ref[...]

    put(own_ref, HALO)

    def halos(below, above):
        put(below, 0)
        put(above, HALO + rows)

    by_side(first_ref, second_ref, halos)

    def line(source, r, field):
        return [source[field, r, :, t * LANES:(t + 1) * LANES] for t in range(tiles)]

    for step in range(SUBSTEPS):
        source, target = (even, odd) if step % 2 == 0 else (odd, even)
        count = extent - 2 - 2 * step

        def finish(field, r, here, ahead, behind):
            for t in range(tiles):
                span = slice(t * LANES, (t + 1) * LANES)
                north, south, east, west, stay = (rates[r, q, :, span] for q in range(5))
                target[field, r, :, span] = (
                    (stay * here[t] + (north * source[field, r + 1, :, span] + south * source[field, r - 1, :, span]))
                    + (east * ahead[t] + west * behind[t])
                )

        def work(first, number, field):
            for r in [first + j for j in range(number)]:
                here = line(source, r, field)
                finish(field, r, here, shifted(here, -1), shifted(here, 1))

        for field in range(chunk):
            def group(index, carry):
                work(step + 1 + ROWS_AT_ONCE * index, ROWS_AT_ONCE, field)
                return carry

            groups, rest = count // ROWS_AT_ONCE, count % ROWS_AT_ONCE
            if groups > 1:
                lax.fori_loop(0, groups, group, 0)
            else:
                work(step + 1, groups * ROWS_AT_ONCE, field)
            work(step + 1 + groups * ROWS_AT_ONCE, rest, field)
    result = even if SUBSTEPS % 2 == 0 else odd

    if not last:
        out_ref[...] = result[:, HALO:HALO + rows]
        return
    sources = [(ref, j, 0) for ref in earlier for j in range(ref.shape[0])]
    sources += [(result, j, HALO) for j in range(chunk)]
    fields = len(sources)
    def mix(f, carry):
        for start in range(0, sector, LANES):
            stop = min(start + LANES, sector)
            for r in range(rows):
                terms = [power_ref[g, f] * ref[j, base + r, :, start:start + LANES]
                         for g, (ref, j, base) in enumerate(sources)]
                stage[start // LANES, r * levels:(r + 1) * levels] = functools.reduce(jnp.add, terms)
            for level in range(levels):
                value = stage[start // LANES, pl.ds(level, rows, stride=levels), :]
                out_ref[f, level, :, start:stop] = value[:, :stop - start]
        return carry

    lax.fori_loop(0, fields, mix, 0)


def lat_pairs(count):
    def both(start):
        ups = [(i, i + 1) for i in range(start, count - 1, 2)]
        return ups + [(j, i) for i, j in ups]

    return both(0), both(1)


def shards(adjoint_in, lat_ahead, lat_behind, lon_ahead, lon_behind, coupling, cutoff):
    fields, levels, rows, sector = adjoint_in.shape
    sectors = lax.axis_size("lon")
    length = sector * sectors
    width = -(-(sector + 2 * HALO) // LANES) * LANES
    even_pairs, odd_pairs = lat_pairs(lax.axis_size("lat"))
    f32 = jnp.float32
    chunks = CHUNKS if sum(CHUNKS) == fields else (fields,)

    def sector_ahead(values, offset):
        return lax.ppermute(values, "lon", [(s, (s - offset) % sectors) for s in range(sectors)])

    def to_bands(first, second):
        return lax.ppermute(first, "lat", even_pairs), lax.ppermute(second, "lat", odd_pairs)

    extent = rows + 2 * HALO
    rate_shape = (RATES, levels, width)
    inputs = [
        pltpu.with_memory_space_constraint(array, pltpu.HBM)
        for array in (adjoint_in, lat_ahead, lat_behind, lon_ahead, lon_behind)
    ]
    payload_shapes = [jax.ShapeDtypeStruct((n, levels, rows, width), f32) for n in chunks]
    later = max(fields - chunks[0], 1)
    first_payload = pl.pallas_call(
        first_pack_kernel,
        out_shape=payload_shapes[0],
        in_specs=[HBM] * (1 + RATES),
        out_specs=VMEM,
        scratch_shapes=[
            pltpu.VMEM((chunks[0],) + adjoint_in.shape[1:], f32),
            pltpu.VMEM((RATES,) + lat_ahead.shape, f32),
            pltpu.SemaphoreType.DMA((1 + RATES,)),
        ],
        compiler_params=PARAMS,
        name="first_pack",
    )(*inputs)
    first_circle = [first_payload] + [sector_ahead(first_payload, k) for k in range(1, sectors)]
    *payloads, rate_own, rate_first, rate_second, limits = pl.pallas_call(
        functools.partial(rest_pack_kernel, chunks),
        out_shape=(
            *payload_shapes[1:],
            jax.ShapeDtypeStruct((rows,) + rate_shape, f32),
            jax.ShapeDtypeStruct((HALO,) + rate_shape, f32),
            jax.ShapeDtypeStruct((HALO,) + rate_shape, f32),
            jax.ShapeDtypeStruct((rows, LANES), f32),
        ),
        in_specs=[HBM] * (2 + RATES),
        out_specs=(VMEM,) * (len(chunks) + 3),
        scratch_shapes=[
            pltpu.VMEM((later,) + adjoint_in.shape[1:], f32),
            pltpu.VMEM((RATES,) + lat_ahead.shape, f32),
            pltpu.SMEM(cutoff.shape, cutoff.dtype),
            pltpu.SemaphoreType.DMA((2 + RATES,)),
        ],
        compiler_params=PARAMS,
        name="rest_pack",
    )(pltpu.with_memory_space_constraint(cutoff, pltpu.HBM), *inputs)
    circles = [[part] + [sector_ahead(part, k) for k in range(1, sectors)] for part in payloads]
    circles.insert(0, first_circle)
    rate_first, rate_second = to_bands(rate_first, rate_second)

    table = jnp.asarray(mode_tables(length))
    results = []
    for c, (n, circle) in enumerate(zip(chunks, circles)):
        lines = n * levels * rows
        is_last = c == len(chunks) - 1
        own, first, second, *power = pl.pallas_call(
            functools.partial(filter_kernel, sectors, c == 0, is_last),
            out_shape=(
                jax.ShapeDtypeStruct((n, rows, levels, width), f32),
                jax.ShapeDtypeStruct((n, HALO, levels, width), f32),
                jax.ShapeDtypeStruct((n, HALO, levels, width), f32),
                *([jax.ShapeDtypeStruct((fields, fields, levels, LANES), f32)] if is_last else []),
            ),
            in_specs=[VMEM] * (sectors + 2 + is_last),
            out_specs=(VMEM,) * (3 + is_last),
            scratch_shapes=[
                pltpu.VMEM((length // LANES, lines, LANES), f32),
                pltpu.VMEM((length // LANES, lines, LANES), f32),
            ],
            compiler_params=PARAMS,
            name="polar_filter",
        )(limits, table, *([jnp.transpose(coupling, (1, 0, 2))] if is_last else []), *circle)
        first, second = to_bands(first, second)
        if c == 0:
            level = pl.pallas_call(
                functools.partial(face_kernel, sector),
                out_shape=jax.ShapeDtypeStruct((extent, 5, levels, width), f32),
                in_specs=[VMEM] * 6,
                out_specs=VMEM,
                compiler_params=PARAMS,
                name="faces",
            )(rate_own, rate_first, rate_second, own, first, second)
        earlier = results if is_last else []
        shape = adjoint_in.shape if is_last else (n, rows, levels, width)
        results.append(pl.pallas_call(
            functools.partial(transport_kernel, n, len(earlier), sector),
            out_shape=jax.ShapeDtypeStruct(shape, f32),
            in_specs=[VMEM] * (5 + len(earlier)),
            out_specs=VMEM,
            scratch_shapes=[
                pltpu.VMEM((n, extent, levels, width), f32),
                pltpu.VMEM((n, extent, levels, width), f32),
                pltpu.VMEM((width // LANES, rows * levels, LANES), f32),
            ],
            compiler_params=PARAMS,
            name="transport",
        )(power[0] if is_last else level, level, own, first, second, *earlier))
    return results[-1]


def solution(mesh):
    placed = (
        P("member", "lev", "lat", "lon"),
        P(("member", "lev"), "lat", "lon"),
        P(("member", "lev"), "lat", "lon"),
        P(("member", "lev"), "lat", "lon"),
        P(("member", "lev"), "lat", "lon"),
        P("lev", None, None),
        P(),
    )
    return jax.shard_map(
        shards,
        mesh=mesh,
        in_specs=placed,
        out_specs=P("member", "lev", "lat", "lon"),
        check_vma=False,
    )
```
